256 devices in a mesh: grp: 2 (over core), gx: 8 (over z), gy: 16 (over x, y).
Axes of the slice: x: 4, y: 4, z: 8, core: 2. Of those that a mesh axis runs over, the one named last changes fastest.
Arguments:
- ocean_state: float32 [4, 60, 128, 2048], P(None, None, ('grp', 'gx'), 'gy'), may hold values from -6 to 6
- diffusivity: float32 [128, 2048], P(('grp', 'gx'), 'gy'), may hold values from 0.03 to 0.24
- wet_mask: int32 [128, 2048], P(('grp', 'gx'), 'gy'), may hold values 0 or 1
- coast_column: int32 [16, 16, 256], P(('grp', 'gx'), 'gy'), may hold values from 0 to 1023, as said below
- coast_slot: int32 [16, 16, 256], P(('grp', 'gx'), 'gy'), may hold values from 0 to 511, as said below
- owner_node: int32 [16, 16, 128, 4], P(('grp', 'gx'), 'gy'), may hold values from -1 to 16383, as said below
- thickness: float32 [2048, 2048], P(('grp', 'gx'), 'gy'), may hold values from 1 to 3
- viscosity: float32 [2048, 2048], P(('grp', 'gx'), 'gy'), may hold values from 0.5 to 2
- friction: float32 [2048, 2048], P(('grp', 'gx'), 'gy'), may hold values from 0.3 to 3
- grounded: int32 [2048, 2048], P(('grp', 'gx'), 'gy'), may hold values 0 or 1
- coupling: float32 [2048, 2048], P(('grp', 'gx'), 'gy'), may hold values from -1 to 1
- driving: float32 [2, 2048, 2048], P(None, ('grp', 'gx'), 'gy'), may hold values from -16 to 16
- first_guess: float32 [2, 2048, 2048], P(None, ('grp', 'gx'), 'gy'), may hold values from -2 to 2
Outputs:
- ocean_next: float32 [4, 60, 128, 2048], P(None, None, ('grp', 'gx'), 'gy')
- melt_mean: float32 [128, 2048], P(('grp', 'gx'), 'gy')
- velocity: float32 [2, 2048, 2048], P(None, ('grp', 'gx'), 'gy')
- residual: float32 [2, 2048, 2048], P(None, ('grp', 'gx'), 'gy')
The draws below stay inside these ranges and needn't reach their ends.
Inputs may be any that keep to these rules, and one draw needn't show every extreme that they name: `coast_column`: within a device the 256 numbers are distinct cells of its block. `coast_slot`: within a device the 256 slots are distinct, so at most 4 items go to one peer; every device sends 4 items to some peer. owner_node of an ice device at (peer p, s) is a node of its block exactly when peer p has an item with slot (this device's peer number) * 4 + s, else -1; the nodes of one device are distinct.
All inputs are finite; a program needn't handle non-finite values. No bound on the sum of `wet_mask` or of `grounded` on one device may be relied on, other than what follows from the above.
Results may differ from the reference program's by a relative error of at most 0.00012.
Values sent between devices are 32-bit elements; how exact they have to be, the bound alone decides.
No kernel may reach another device: no remote copies, remote signals or barrier semaphores. Data moves between devices by JAX's collectives and lax.ppermute only.
A program may use at most 64 MiB of HBM per device.

```python
import math
import jax
import jax.numpy as jnp

LEV = 60
CX = 8
CY = 128
IX = 128
NSUB = 4
ITERS = 2
CAP = 4
XB = 16
YB = 16
PEERS = 128
G_DEV = 256
OX = 128
OY = 2048
NXI = 2048
N_GX = 8
N_GY = 16


def coast_lists(key):
    base = jax.random.fold_in(key, 41)
    device_count = XB * YB
    slot_count = PEERS * CAP

    def one_device(device_key):
        key_order, key_full, key_cols, key_nodes = jax.random.split(device_key, 4)
        priority = jax.random.permutation(key_order, slot_count)
        full_peer = jax.random.randint(key_full, (), 0, PEERS)
        priority = jnp.where(jnp.arange(slot_count) // CAP == full_peer, priority - slot_count, priority)
        chosen = jnp.argsort(priority)[:G_DEV]
        columns = jax.random.permutation(key_cols, CX * CY)[:G_DEV]
        nodes = jax.random.permutation(key_nodes, IX * CY)[:slot_count]
        return (chosen.astype(jnp.int32), columns.astype(jnp.int32), nodes.astype(jnp.int32))
    chosen, columns, nodes = jax.vmap(one_device)(jax.random.split(base, device_count))
    used = jnp.zeros((device_count, slot_count), jnp.int32).at[jnp.arange(device_count)[:, None], chosen].set(1)
    halves = device_count // PEERS
    used = used.reshape(halves, PEERS, PEERS, CAP).transpose(0, 2, 1, 3).reshape(device_count, slot_count)
    owners = jnp.where(used == 1, nodes, -1).astype(jnp.int32)
    return (chosen.reshape(XB, YB, G_DEV), columns.reshape(XB, YB, G_DEV), owners.reshape(XB, YB, PEERS, CAP))


def draw_coast_slot(key, part):
    return coast_lists(key)[0]


def draw_coast_column(key, part):
    return coast_lists(key)[1]


def draw_owner_node(key, part):
    return coast_lists(key)[2]


def draw_driving(key, part):
    row_share = jnp.arange(NXI, dtype=jnp.float32) / max(NXI - 1, 1)
    rise_rows = 3.0 ** row_share
    noise = jnp.clip(jax.random.normal(key, (2, NXI, OY), jnp.float32), -4.0, 4.0)
    return noise * rise_rows[:, None]


def touch_ends(entries, key, least, high):
    dims = entries.shape
    place = [jax.random.randint(jax.random.fold_in(key, axis), (), 0, dims[axis]) for axis in range(len(dims))]
    entries = entries.at[tuple(place)].set(least)
    longest = dims.index(max(dims))
    place[longest] = (place[longest] + 1) % dims[longest]
    return entries.at[tuple(place)].set(high)


def shard_levels(key, shape, shards, least, top_value):
    gain = 1.0
    for axis_at, shards_of in shards:
        steps = jax.random.uniform(jax.random.fold_in(jax.random.fold_in(key, 6), axis_at), (shards_of,), jnp.float32, least / len(shards), top_value / len(shards))
        gain = gain * jnp.repeat(jnp.exp(steps), shape[axis_at] // shards_of).reshape((-1,) + (1,) * (len(shape) - 1 - axis_at))
    return gain


def centred(own_key, shape, width, reach, pieces=(), held_as=jnp.bfloat16):
    gain = shard_levels(own_key, shape, pieces, -0.22, 0.18) if pieces else 1.0
    drawn = jax.random.normal(own_key, shape, jnp.float32) * width * gain
    return jnp.minimum(jnp.maximum(drawn, -reach), reach).astype(held_as)


def setup_inputs(seed: int = 0) -> dict:
    key_list = jax.random.split(jax.random.key(seed), 14)
    ocean_state = centred(key_list[0], (4, LEV, OX, OY), 1.0, 6.0, ((2, 16), (3, 16)), jnp.float32)
    diffusivity = jnp.clip(jnp.exp(math.log(0.24) - 2.0794415 * jax.random.uniform(key_list[1], (OX, OY), jnp.float32) ** shard_levels(key_list[1], (OX, OY), ((0, 16), (1, 16)), -0.2, 0.2)), 0.03, 0.24)
    wet_mask = touch_ends((jax.random.randint(key_list[2], (OX, OY), 0, 8) < 7).astype(jnp.int32), jax.random.fold_in(key_list[2], 1), 0, 1)
    coast_column = draw_coast_column(jax.random.fold_in(key_list[13], 71), 0)
    coast_slot = draw_coast_slot(jax.random.fold_in(key_list[13], 71), 0)
    owner_node = draw_owner_node(jax.random.fold_in(key_list[13], 71), 0)
    thickness = jnp.clip(jnp.exp(math.log(3.0) - 1.0986123 * jax.random.uniform(key_list[6], (NXI, OY), jnp.float32) ** shard_levels(key_list[6], (NXI, OY), ((0, 16), (1, 16)), -0.2, 0.2)), 1.0, 3.0)
    viscosity = jnp.clip(jnp.exp(math.log(2.0) - 1.3862944 * jax.random.uniform(key_list[7], (NXI, OY), jnp.float32) ** shard_levels(key_list[7], (NXI, OY), ((0, 16), (1, 16)), -0.2, 0.2)), 0.5, 2.0)
    friction = jnp.clip(jnp.exp(math.log(3.0) - 2.3025851 * jax.random.uniform(key_list[8], (NXI, OY), jnp.float32) ** shard_levels(key_list[8], (NXI, OY), ((0, 16), (1, 16)), -0.2, 0.2)), 0.3, 3.0)
    grounded = touch_ends((jax.random.randint(key_list[9], (NXI, OY), 0, 2) < 1).astype(jnp.int32), jax.random.fold_in(key_list[9], 1), 0, 1)
    coupling = jnp.clip(jax.random.uniform(key_list[10], (NXI, OY), jnp.float32, -1.0, 1.0) * shard_levels(key_list[10], (NXI, OY), ((0, 16), (1, 16)), -0.4, 0.0), -1.0, 1.0)
    driving = draw_driving(jax.random.fold_in(key_list[13], 71), 0)
    first_guess = centred(key_list[12], (2, NXI, OY), 0.3, 2.0, ((1, 16), (2, 16)), jnp.float32)
    return {"ocean_state": ocean_state, "diffusivity": diffusivity, "wet_mask": wet_mask, "coast_column": coast_column, "coast_slot": coast_slot, "owner_node": owner_node, "thickness": thickness, "viscosity": viscosity, "friction": friction, "grounded": grounded, "coupling": coupling, "driving": driving, "first_guess": first_guess}


def advance(padded, diff_pad, wet_pad, cover, draft_field):
    fields = padded[:, :, 1:-1, 1:-1]
    row_total = fields.shape[2]
    col_total = fields.shape[3]
    diff_here = diff_pad[1:-1, 1:-1]
    wet_here = wet_pad[1:-1, 1:-1]
    flux_sum = jnp.zeros_like(fields)
    for offset in ((2, 1), (0, 1), (1, 2), (1, 0)):
        diff_side = diff_pad[offset[0]:offset[0] + row_total, offset[1]:offset[1] + col_total]
        wet_side = wet_pad[offset[0]:offset[0] + row_total, offset[1]:offset[1] + col_total]
        side_vals = padded[:, :, offset[0]:offset[0] + row_total, offset[1]:offset[1] + col_total]
        weight = 0.5 * (diff_here + diff_side) * wet_here * wet_side
        flux_sum = flux_sum + weight * (side_vals - fields)
    top_temp = fields[0, 0]
    top_salt = fields[1, 0]
    top_east = fields[2, 0]
    top_north = fields[3, 0]
    current_speed = jnp.sqrt(top_east * top_east + top_north * top_north + 0.01)
    freezing = -0.5 * top_salt + 0.3 * draft_field - 0.2
    melt_rate = 0.5 * cover * (top_temp - freezing) * current_speed
    updated = fields + flux_sum
    drag_rate = 0.05 * cover * current_speed
    top_rows = jnp.stack([updated[0, 0] - 0.3 * melt_rate, updated[1, 0] - 0.2 * melt_rate, updated[2, 0] - drag_rate * top_east, updated[3, 0] - drag_rate * top_north])
    updated = updated.at[:, 0].set(top_rows)
    return (updated, melt_rate)

def operator_parts(depth_visc, visc_pad, friction, grounded, coupling):
    weight_east = 0.5 * (depth_visc + visc_pad[2:, 1:-1])
    weight_west = 0.5 * (depth_visc + visc_pad[:-2, 1:-1])
    weight_north = 0.5 * (depth_visc + visc_pad[1:-1, 2:])
    weight_south = 0.5 * (depth_visc + visc_pad[1:-1, :-2])
    base_friction = friction * grounded.astype(jnp.float32) + 0.2
    cross_term = 0.9 * base_friction * coupling
    diagonal = weight_east + weight_west + weight_north + weight_south + base_friction
    return (diagonal, weight_east, weight_west, weight_north, weight_south, cross_term)

def apply_padded(vector_pad, parts):
    diagonal, weight_east, weight_west, weight_north, weight_south, cross_term = parts
    inner = vector_pad[:, 1:-1, 1:-1]
    beside = weight_east * vector_pad[:, 2:, 1:-1] + weight_west * vector_pad[:, :-2, 1:-1]
    beside = beside + weight_north * vector_pad[:, 1:-1, 2:] + weight_south * vector_pad[:, 1:-1, :-2]
    return diagonal * inner - beside + cross_term * inner[::-1]

def pad_vector(vector):
    return jnp.pad(vector, ((0, 0), (1, 1), (1, 1)))

def to_blocks(grid_field, row_count):
    return grid_field.reshape(XB, row_count, YB, CY).transpose(0, 2, 1, 3).reshape(XB, YB, row_count * CY)

def from_blocks(blocks, row_count):
    return blocks.reshape(XB, YB, row_count, CY).transpose(0, 2, 1, 3).reshape(XB * row_count, YB * CY)

def reference(ocean_state, diffusivity, wet_mask, coast_column, coast_slot, owner_node, thickness, viscosity, friction, grounded, coupling, driving, first_guess):
    block_x = jnp.broadcast_to(jnp.arange(XB, dtype=jnp.int32)[:, None, None], coast_slot.shape)
    block_y = jnp.broadcast_to(jnp.arange(YB, dtype=jnp.int32)[None, :, None], coast_slot.shape)
    peer_index = coast_slot // CAP
    slot_index = coast_slot % CAP
    owner_x = block_x // N_GX * N_GX + peer_index // N_GY
    owner_y = peer_index % N_GY
    sender = block_x % N_GX * N_GY + block_y
    node_index = owner_node[owner_x, owner_y, sender, slot_index]
    thick_blocks = to_blocks(thickness, IX)
    draft_item = 0.9 * thick_blocks[owner_x, owner_y, node_index]
    cover_blocks = jnp.zeros((XB, YB, CX * CY), jnp.float32).at[block_x, block_y, coast_column].set(1.0)
    draft_blocks = jnp.zeros((XB, YB, CX * CY), jnp.float32).at[block_x, block_y, coast_column].set(draft_item)
    cover = from_blocks(cover_blocks, CX)
    draft_field = from_blocks(draft_blocks, CX)
    diff_pad = jnp.pad(diffusivity, 1)
    wet_pad = jnp.pad(wet_mask.astype(jnp.float32), 1)
    fields = ocean_state
    total = jnp.zeros((OX, OY), jnp.float32)
    for substep in range(NSUB):
        padded = jnp.pad(fields, ((0, 0), (0, 0), (1, 1), (1, 1)))
        fields, melt_rate = advance(padded, diff_pad, wet_pad, cover, draft_field)
        total = total + melt_rate
    melt_mean = total / NSUB
    melt_item = to_blocks(melt_mean, CX)[block_x, block_y, coast_column]
    melt_node = jnp.zeros((XB, YB, IX * CY), jnp.float32).at[owner_x, owner_y, node_index].add(melt_item)
    thinned = thickness * jnp.exp(-0.3 * from_blocks(melt_node, IX))
    depth_visc = viscosity * thinned
    parts = operator_parts(depth_visc, jnp.pad(depth_visc, 1), friction, grounded, coupling)
    rhs = driving * thinned
    velocity = first_guess
    residual = rhs - apply_padded(pad_vector(first_guess), parts)
    precond = residual / parts[0]
    direction = precond
    norm_now = jnp.sum(residual * precond)
    for iteration in range(ITERS):
        image = apply_padded(pad_vector(direction), parts)
        step_size = norm_now / jnp.sum(direction * image)
        velocity = velocity + step_size * direction
        residual = residual - step_size * image
        if iteration + 1 < ITERS:
            precond = residual / parts[0]
            norm_next = jnp.sum(residual * precond)
            direction = precond + norm_next / norm_now * direction
            norm_now = norm_next
    return (fields, melt_mean, velocity, residual)
```

```python
import jax
import jax.numpy as jnp
from jax import lax
from jax.experimental import pallas as pl
from jax.experimental.pallas import tpu as pltpu
from jax.sharding import Mesh
from jax.sharding import PartitionSpec as P

NSUB = 4
HALO = 4
GY = ("gy_0", "gy_1")
XAXES = ("grp", "gx")
ALL = ("grp", "gx", "gy_0", "gy_1")
LEAD = 24
F32 = jnp.float32
BF16 = jnp.bfloat16
I32 = jnp.int32


def iota(shape, dim):
    return lax.broadcasted_iota(I32, shape, dim)


def split3(x):
    high = x.astype(BF16)
    rest = x - high.astype(F32)
    mid = rest.astype(BF16)
    low = (rest - mid.astype(F32)).astype(BF16)
    return high, mid, low


def onehot(hit):
    return jnp.where(hit, 1.0, 0.0).astype(BF16)


def dot_tn(a, b):
    return lax.dot_general(a, b, (((0,), (0,)), ((), ())), preferred_element_type=F32)


def dot_nt(a, b):
    return lax.dot_general(a, b, (((1,), (1,)), ((), ())), preferred_element_type=F32)


def spread(table, half, out_ref):
    row = iota((128, 128), 0) & 15
    group = iota((128, 128), 1) >> 2
    after = pltpu.roll(table, 127, 0)
    before = pltpu.roll(table, 1, 0)
    parts = []
    for dx in range(3):
        part = jnp.where((group == 3 * dx) & (row > 0), before, 0.0)
        part = jnp.where(group == 3 * dx + 1, table, part)
        part = jnp.where((group == 3 * dx + 2) & (row < 15), after, part)
        parts.append(part)
    none = jnp.zeros((16, 128), F32)
    own = parts[1] + jnp.concatenate([none, parts[0][:112]], 0)
    own = own + jnp.concatenate([parts[2][16:], none], 0)
    first = jnp.where(half == 0, parts[0][112:], 0.0)
    last = jnp.where(half == 1, parts[2][:16], 0.0)
    out_ref[pl.ds(half * 128, 128), :] = own
    out_ref[pl.ds((1 - half) * 128, 128), :] = jnp.concatenate(
        [first, jnp.zeros((96, 128), F32), last], 0
    )


def draft_kernel(pos_ref, owner_ref, thick_ref, out_ref):
    lane = iota((128, 128), 1)
    parts = split3(thick_ref[...])
    node = owner_ref[...]
    table = jnp.zeros((128, 128), F32)
    for s in range(4):
        column = node[:, s : s + 1]
        pick = onehot(lane == (column >> 7))
        rows = jnp.dot(pick, parts[0], preferred_element_type=F32)
        rows = rows + jnp.dot(pick, parts[1], preferred_element_type=F32)
        rows = rows + jnp.dot(pick, parts[2], preferred_element_type=F32)
        value = jnp.sum(jnp.where(lane == (column & 127), rows, 0.0), 1, keepdims=True)
        table = jnp.where((lane & 3) == s, 0.9 * value, table)
    spread(table, pos_ref[0], out_ref)


def ice_fields(refs):
    thick, visc, fric, ground, coup, drive, guess = refs
    return (
        lambda at: thick[at],
        lambda at: visc[at],
        lambda at: fric[at] * ground[at].astype(F32),
        lambda at: coup[at],
        lambda at: drive[(0,) + at],
        lambda at: drive[(1,) + at],
        lambda at: guess[(0,) + at],
        lambda at: guess[(1,) + at],
    )


def pack_x_kernel(
    state_ref, diff_ref, wet_ref, col_ref, slot_ref, owner_ref,
    thick, visc, fric, ground, coup, drive, guess,
    up_ref, down_ref, slotmap_ref, nodemap_ref,
):
    col = col_ref[...]
    slot = slot_ref[...]
    hit = iota((8, 256), 0) == (col >> 7)
    peer = jnp.where(hit, ((slot >> 2) + 1).astype(F32), 0.0)
    which = jnp.where(hit, (slot & 3).astype(F32), 0.0)
    lanes = onehot(iota((128, 256), 0) == (col & 127))
    both = dot_nt(jnp.concatenate([peer, which], 0).astype(BF16), lanes)
    slotmap = jnp.where(both[:8] > 0.5, 4.0 * both[:8] + both[8:] - 3.0, 0.0)
    slotmap_ref[...] = slotmap

    node = owner_ref[...]
    lane = iota((128, 128), 1)
    number = iota((128, 128), 0).astype(F32) + 1.0
    peers = []
    whichs = []
    cols = []
    for s in range(4):
        column = node[:, s : s + 1]
        hit = lane == (column >> 7)
        peers.append(jnp.where(hit, number, 0.0).astype(BF16))
        whichs.append(jnp.where(hit, float(s), 0.0).astype(BF16))
        cols.append(onehot(lane == (column & 127)))
    cols = jnp.concatenate(cols, 0)
    peer = dot_tn(jnp.concatenate(peers, 0), cols)
    which = dot_tn(jnp.concatenate(whichs, 0), cols)
    nodemap_ref[...] = jnp.where(peer > 0.5, 4.0 * peer + which - 3.0, 0.0)

    for f in range(4):
        up_ref[f] = state_ref[f, 0, 4:8]
        down_ref[f] = state_ref[f, 0, 0:4]
        up_ref[LEAD + 59 * f : LEAD + 59 * f + 59] = state_ref[f, 1:, 4:8]
        down_ref[LEAD + 59 * f : LEAD + 59 * f + 59] = state_ref[f, 1:, 0:4]
    up_ref[4] = diff_ref[4:8]
    down_ref[4] = diff_ref[0:4]
    wet = wet_ref[...].astype(F32)
    up_ref[5] = wet[4:8]
    down_ref[5] = wet[0:4]
    up_ref[6] = slotmap[4:8]
    down_ref[6] = slotmap[0:4]
    up_ref[7] = jnp.zeros((4, 128), F32)
    down_ref[7] = jnp.zeros((4, 128), F32)
    top = (pl.ds(0, 4), slice(None))
    end = (pl.ds(124, 4), slice(None))
    for a, get in enumerate(ice_fields((thick, visc, fric, ground, coup, drive, guess))):
        up_ref[8 + a] = get(end)
        down_ref[8 + a] = get(top)
    up_ref[16] = nodemap_ref[124:128]
    down_ref[16] = nodemap_ref[0:4]
    for a in range(17, LEAD):
        up_ref[a] = jnp.zeros((4, 128), F32)
        down_ref[a] = jnp.zeros((4, 128), F32)


def pack_y_kernel(
    state_ref, diff_ref, wet_ref, slotmap_ref, lo_ref, hi_ref,
    thick, visc, fric, ground, coup, drive, guess, nodemap_ref,
    up_ref, down_ref,
):
    lane = iota((16, 128), 1)
    at_first = lane >> 2
    at_last = ((lane + 4) & 127) >> 2

    def add(i, own, entry, acc):
        whole = jnp.concatenate([own, hi_ref[entry], lo_ref[entry]], 0)
        rolled = whole if i == 0 else pltpu.roll(whole, 4 * i, 1)
        return (
            jnp.where(at_last == i, rolled, acc[0]),
            jnp.where(at_first == i, rolled, acc[1]),
        )

    for group in range(8):
        acc = (jnp.zeros((16, 128), F32), jnp.zeros((16, 128), F32))
        for i in range(32):
            index = group * 32 + i
            if index < 4:
                acc = add(i, state_ref[index, 0], index, acc)
            elif index == 4:
                acc = add(i, diff_ref[...], index, acc)
            elif index == 5:
                acc = add(i, wet_ref[...].astype(F32), index, acc)
            elif index == 6:
                acc = add(i, slotmap_ref[...], index, acc)
            elif 8 <= index < 244:
                b = index - 8
                acc = add(i, state_ref[b // 59, b % 59 + 1], LEAD + b, acc)
        up_ref[16 * group : 16 * group + 16] = acc[0]
        down_ref[16 * group : 16 * group + 16] = acc[1]

    lane = iota((136, 128), 1)
    at_first = lane >> 2
    at_last = ((lane + 4) & 127) >> 2
    last = jnp.zeros((136, 128), F32)
    first = jnp.zeros((136, 128), F32)
    whole_at = (slice(None), slice(None))
    gets = ice_fields((thick, visc, fric, ground, coup, drive, guess))
    gets = gets + (lambda at: nodemap_ref[...],)
    for a, get in enumerate(gets):
        whole = jnp.concatenate([get(whole_at), hi_ref[8 + a], lo_ref[8 + a]], 0)
        rolled = whole if a == 0 else pltpu.roll(whole, 4 * a, 1)
        last = jnp.where(at_last == a, rolled, last)
        first = jnp.where(at_first == a, rolled, first)
    up_ref[128:264] = last
    down_ref[128:264] = first


def side_lanes(left, right, i, keep):
    lane = iota(left.shape, 1)
    both = jnp.where(((lane + 4) & 127) >> 2 == i, left, right)
    both = pltpu.roll(both, 128 - 4 * i, 1) if i else both
    return jnp.where((lane < 4) | (lane >= 124), both, 0.0) if keep else both


def turn(x, shift, axis):
    return pltpu.roll(x, shift % x.shape[axis], axis)


def lookup(parts, owner, lane_of):
    pick = onehot(iota((256, 128), 0) == owner)
    found = jnp.dot(parts, pick, preferred_element_type=F32)
    found = found[0:48] + found[48:96] + found[96:144]
    return jnp.sum(jnp.where(iota((48, 128), 0) == lane_of, found, 0.0), 0, keepdims=True)


def table_parts(table):
    turned = jnp.transpose(table)[0:48]
    return jnp.concatenate(split3(turned), 0)


def decode(code, half, group):
    number = code.astype(I32) - 1
    owner = jnp.where(number >= 0, half * 128 + (number >> 2), -1)
    return owner, 4 * group + (number & 3)


def pack_rows(x):
    lane = iota((16, 128), 1)
    moved = jnp.where(lane < 8, pltpu.roll(x, 4, 1), 0.0)
    moved = pltpu.roll(moved, 0, 1, stride=8, stride_axis=0)
    return jnp.sum(moved, 0, keepdims=True)


def unpack_rows(row):
    lane = iota((16, 128), 1)
    turned = [row] + [pltpu.roll(row, 128 - 8 * r, 1) for r in range(1, 16)]
    moved = jnp.where(lane < 8, jnp.concatenate(turned, 0), 0.0)
    return pltpu.roll(moved, 124, 1)


def top_kernel(
    pos_ref, state_ref, diff_ref, wet_ref, slotmap_ref, lo_ref, hi_ref, left_ref, right_ref, table_ref,
    top_ref, melt_ref, weight_ref, send_ref,
):
    half = pos_ref[0]
    half_lo = pos_ref[1]
    half_hi = pos_ref[2]
    left = left_ref[0:16]
    right = right_ref[0:16]

    def padded(i, own):
        centre = jnp.concatenate([own, hi_ref[i], lo_ref[i]], 0)
        return jnp.concatenate([centre, side_lanes(left, right, i, True)], 1)

    fields = [padded(f, state_ref[f, 0]) for f in range(4)]
    diff = padded(4, diff_ref[...])
    wet = padded(5, wet_ref[...].astype(F32))
    code = padded(6, slotmap_ref[...])
    weights = []
    for axis, shift in ((0, -1), (0, 1), (1, -1), (1, 1)):
        weights.append(0.5 * (diff + turn(diff, shift, axis)) * wet * turn(wet, shift, axis))
    for j in range(4):
        weight_ref[j] = weights[j]
    weight_ref[4] = 1.0 - (weights[0] + weights[1] + weights[2] + weights[3])

    row = iota((16, 256), 0)
    col = iota((16, 256), 1)
    half_at = jnp.where(row < 8, half, jnp.where(row < 12, half_hi, half_lo))
    dx = jnp.where(row < 8, 1, jnp.where(row < 12, 2, 0))
    dy = jnp.where(col < 128, 1, jnp.where(col < 192, 2, 0))
    owner, lane_of = decode(code, half_at, 3 * dx + dy)
    side_owner = (pack_rows((owner[:, 128:] + 1).astype(F32))).astype(I32) - 1
    side_lane = pack_rows(lane_of[:, 128:].astype(F32)).astype(I32)
    parts = table_parts(table_ref[...])
    found = [lookup(parts, owner[r : r + 1, :128], lane_of[r : r + 1, :128]) for r in range(16)]
    side = unpack_rows(lookup(parts, side_owner, side_lane))
    draft = jnp.concatenate([jnp.concatenate(found, 0), side], 1)
    cover = jnp.where(code > 0.5, 1.0, 0.0)

    total = jnp.zeros((8, 128), F32)
    for substep in range(NSUB):
        temp, salt, east, north = fields
        speed = jnp.sqrt(east * east + north * north + 0.01)
        freezing = -0.5 * salt + 0.3 * draft - 0.2
        melt = 0.5 * cover * (temp - freezing) * speed
        drag = 0.05 * cover * speed
        total = total + melt[0:8, 0:128]
        loss = (0.3 * melt, 0.2 * melt, drag * east, drag * north)
        changed = []
        for f in range(4):
            x = fields[f]
            flux = weights[0] * (turn(x, -1, 0) - x) + weights[1] * (turn(x, 1, 0) - x)
            flux = flux + weights[2] * (turn(x, -1, 1) - x) + weights[3] * (turn(x, 1, 1) - x)
            changed.append(x + flux - loss[f])
        fields = changed
    for f in range(4):
        top_ref[f] = fields[f][0:8, 0:128]
    mean = total * (1.0 / NSUB)
    melt_ref[...] = mean

    number = slotmap_ref[...].astype(I32) - 1
    peers = []
    values = []
    for r in range(8):
        at = number[r : r + 1]
        peers.append(onehot(iota((128, 128), 0) == (at >> 2)))
        values.append(jnp.where((iota((128, 128), 0) & 3) == (at & 3), mean[r : r + 1], 0.0))
    peers = jnp.concatenate(peers, 1)
    values = jnp.concatenate(split3(jnp.concatenate(values, 1)), 0)
    table = dot_nt(peers, values)
    spread(table[:, 0:128] + table[:, 128:256] + table[:, 256:384], half, send_ref)


def bulk_kernel(
    state_ref, lo_ref, hi_ref, left_ref, right_ref, weight_ref, top_ref, out_ref,
):
    for f in range(4):
        out_ref[f, 0] = top_ref[f]
    lane = iota((16, 128), 1)
    last_group = ((lane + 4) & 127) >> 2

    def level(step, carry):
        for f in range(4):
            b = 59 * f + step
            index = b + 8
            i = index & 31
            at = pl.multiple_of((index >> 5) * 16, 16)
            left = left_ref[pl.ds(at, 16), :]
            right = right_ref[pl.ds(at, 16), :]
            both = pltpu.roll(jnp.where(last_group == i, left, right), (128 - 4 * i) & 127, 1)
            centre = jnp.concatenate([state_ref[f, step + 1], hi_ref[LEAD + b], lo_ref[LEAD + b]], 0)
            x = jnp.concatenate([centre, both], 1)
            for substep in range(NSUB):
                y = weight_ref[4] * x
                y = y + weight_ref[0] * turn(x, -1, 0) + weight_ref[1] * turn(x, 1, 0)
                x = y + weight_ref[2] * turn(x, -1, 1) + weight_ref[3] * turn(x, 1, 1)
            out_ref[f, step + 1] = x[0:8, 0:128]
        return carry

    lax.fori_loop(0, 59, level, 0)


def ice_kernel(
    pos_ref, owner_ref, table_ref, lo_ref, hi_ref, left_ref, right_ref,
    thick, visc, fric, ground, coup, drive, guess, nodemap_ref,
    send_ref, res_ref, z_ref, y_ref, w_ref, v_ref,
):
    half = pos_ref[0]
    half_lo = pos_ref[1]
    half_hi = pos_ref[2]
    left = left_ref[...]
    right = right_ref[...]
    whole_at = (slice(None), slice(None))

    gets = ice_fields((thick, visc, fric, ground, coup, drive, guess))
    gets = gets + (lambda at: nodemap_ref[...],)

    def padded(a):
        centre = jnp.concatenate([gets[a](whole_at), hi_ref[8 + a], lo_ref[8 + a]], 0)
        return jnp.concatenate([centre, side_lanes(left, right, a, True)], 1)

    table = table_ref[...]
    mine = table_ref[pl.ds(half * 128, 128), :]
    node = owner_ref[...]
    lane = iota((128, 128), 1)
    rows = []
    cols = []
    for s in range(4):
        column = node[:, s : s + 1]
        rows.append(onehot(lane == (column >> 7)))
        cols.append(jnp.where(lane == (column & 127), mine[:, 16 + s : 17 + s], 0.0))
    cols = jnp.concatenate(split3(jnp.concatenate(cols, 0)), 1)
    melt = dot_tn(jnp.concatenate(rows, 0), cols)
    melt = melt[:, 0:128] + melt[:, 128:256] + melt[:, 256:384]

    code = padded(8)
    row = iota((136, 256), 0)
    col = iota((136, 256), 1)
    half_at = jnp.where(row < 128, half, jnp.where(row < 132, half_hi, half_lo))
    dx = jnp.where(row < 128, 1, jnp.where(row < 132, 2, 0))
    dy = jnp.where(col < 128, 1, jnp.where(col < 192, 2, 0))
    owner, lane_of = decode(code, half_at, 3 * dx + dy)
    parts = table_parts(table)
    rim = [
        lookup(parts, owner[r : r + 1, :128], lane_of[r : r + 1, :128]) for r in range(128, 136)
    ]
    side_owner = (owner[:, 128:] + 1).astype(F32)
    side_lane = lane_of[:, 128:].astype(F32)
    spare = jnp.zeros((8, 128), F32)
    sides = []
    for block in range(9):
        if block < 8:
            piece_owner = side_owner[16 * block : 16 * block + 16]
            piece_lane = side_lane[16 * block : 16 * block + 16]
        else:
            piece_owner = jnp.concatenate([side_owner[128:136], spare], 0)
            piece_lane = jnp.concatenate([side_lane[128:136], spare], 0)
        at_owner = pack_rows(piece_owner).astype(I32) - 1
        at_lane = pack_rows(piece_lane).astype(I32)
        piece = unpack_rows(lookup(parts, at_owner, at_lane))
        sides.append(piece if block < 8 else piece[0:8])
    melt = jnp.concatenate([melt] + rim, 0)
    melt = jnp.concatenate([melt, jnp.concatenate(sides, 0)], 1)

    thickness = padded(0)
    inside = thickness > 0.0
    thinned = thickness * jnp.exp(-0.3 * melt)
    depth = padded(1) * thinned
    base = padded(2) + 0.2
    cross = 0.9 * base * padded(3)
    w_e = 0.5 * (depth + turn(depth, -1, 0))
    w_w = 0.5 * (depth + turn(depth, 1, 0))
    w_n = 0.5 * (depth + turn(depth, -1, 1))
    w_s = 0.5 * (depth + turn(depth, 1, 1))
    diagonal = w_e + w_w + w_n + w_s + base
    inverse = jnp.where(inside, 1.0 / diagonal, 0.0)

    def apply(pair):
        out = []
        for a in range(2):
            x = pair[a]
            beside = w_e * turn(x, -1, 0) + w_w * turn(x, 1, 0)
            beside = beside + w_n * turn(x, -1, 1) + w_s * turn(x, 1, 1)
            out.append(diagonal * x - beside + cross * pair[1 - a])
        return out

    first = [padded(6), padded(7)]
    image = apply(first)
    res = [padded(4 + a) * thinned - image[a] for a in range(2)]
    z = [res[a] * inverse for a in range(2)]
    y = apply(z)
    w = [y[a] * inverse for a in range(2)]
    v = apply(w)
    inner = (slice(0, 128), slice(0, 128))
    sums = []
    for one, two in ((res, z), (z, y), (y, w), (w, v)):
        product = one[0][inner] * two[0][inner] + one[1][inner] * two[1][inner]
        sums.append(jnp.sum(jnp.sum(product, 0, keepdims=True), 1, keepdims=True))
    lane = iota((256, 128), 1)
    message = jnp.zeros((256, 128), F32)
    for k in range(4):
        message = jnp.where(lane == k, sums[k], message)
    send_ref[...] = message
    for a in range(2):
        res_ref[a] = res[a][inner]
        z_ref[a] = z[a][inner]
        y_ref[a] = y[a][inner]
        w_ref[a] = w[a][inner]
        v_ref[a] = v[a][inner]


def update_kernel(sum_ref, guess_ref, res_ref, z_ref, y_ref, w_ref, v_ref, vel_ref, left_ref):
    total = jnp.sum(sum_ref[...], 0, keepdims=True)
    norm, curve, mixed, far = (total[:, k : k + 1] for k in range(4))
    step = norm / curve
    norm_next = norm - 2.0 * step * curve + step * step * mixed
    ratio = norm_next / norm
    along = curve - step * mixed
    curve_next = curve - 2.0 * step * mixed + step * step * far
    curve_next = curve_next + 2.0 * ratio * along + ratio * ratio * curve
    step_next = norm_next / curve_next
    one = step + step_next * (1.0 + ratio)
    two = step_next * step
    for a in range(2):
        vel_ref[a] = guess_ref[a] + one * z_ref[a] - two * w_ref[a]
        left_ref[a] = res_ref[a] - one * y_ref[a] + two * v_ref[a]


def sds(*shape):
    return jax.ShapeDtypeStruct(shape, F32)


SMEM = pl.BlockSpec(memory_space=pltpu.SMEM)


def whole(*shape):
    return pl.BlockSpec(shape, lambda *_: (0,) * len(shape))


def call(kernel, name, in_specs, outs, **kw):
    return pl.pallas_call(
        kernel,
        name=name,
        grid=(1,),
        in_specs=in_specs,
        out_specs=[whole(*o.shape) for o in outs],
        out_shape=outs,
        **kw,
    )


def swap(value, axes, dim_up):
    size = lax.axis_size(axes)
    forward = [(i, i + 1) for i in range(size - 1)]
    up, down = dim_up
    low = lax.ppermute(up, axes, forward)
    high = lax.ppermute(down, axes, [(b, a) for a, b in forward])
    return low, high


def exchange(table):
    return lax.all_to_all(table, ALL, split_axis=0, concat_axis=0, tiled=True)


def shards(
    ocean_state, diffusivity, wet_mask, coast_column, coast_slot, owner_node,
    thickness, viscosity, friction, grounded, coupling, driving, first_guess,
):
    grp = lax.axis_index("grp")
    bx = grp * 8 + lax.axis_index("gx")
    pos = jnp.stack([grp, jnp.maximum(bx - 1, 0) // 8, jnp.minimum(bx + 1, 15) // 8]).astype(I32)
    owner = owner_node[0, 0]
    columns = coast_column.reshape(1, 256)
    slots = coast_slot.reshape(1, 256)
    ice = (thickness, viscosity, friction, grounded, coupling, driving, first_guess)
    ice_specs = [whole(128, 128)] * 5 + [whole(2, 128, 128)] * 2
    state_spec = whole(4, 60, 8, 128)
    entries = LEAD + 236

    (send_draft,) = call(
        draft_kernel, "draft", [SMEM, whole(128, 4), whole(128, 128)], [sds(256, 128)]
    )(pos, owner, thickness)
    up, down, slotmap, nodemap = call(
        pack_x_kernel,
        "pack_x",
        [state_spec, whole(8, 128), whole(8, 128), whole(1, 256), whole(1, 256), whole(128, 4)] + ice_specs,
        [sds(entries, 4, 128), sds(entries, 4, 128), sds(8, 128), sds(128, 128)],
    )(ocean_state, diffusivity, wet_mask, columns, slots, owner, *ice)
    lo, hi = swap(None, XAXES, (up, down))
    got_draft = exchange(send_draft)
    up, down = call(
        pack_y_kernel,
        "pack_y",
        [state_spec, whole(8, 128), whole(8, 128), whole(8, 128), whole(entries, 4, 128), whole(entries, 4, 128)]
        + ice_specs
        + [whole(128, 128)],
        [sds(264, 128), sds(264, 128)],
    )(ocean_state, diffusivity, wet_mask, slotmap, lo, hi, *ice, nodemap)
    left, right = swap(None, GY, (up, down))

    top, melt_mean, weights, send_melt = call(
        top_kernel,
        "top",
        [SMEM, whole(4, 1, 8, 128), whole(8, 128), whole(8, 128), whole(8, 128), whole(8, 4, 128), whole(8, 4, 128)]
        + [whole(16, 128), whole(16, 128), whole(256, 128)],
        [sds(4, 8, 128), sds(8, 128), sds(5, 16, 256), sds(256, 128)],
    )(pos, ocean_state, diffusivity, wet_mask, slotmap, lo, hi, left, right, got_draft)
    got_melt = exchange(send_melt)
    (fields,) = call(
        bulk_kernel,
        "bulk",
        [state_spec, whole(entries, 4, 128), whole(entries, 4, 128), whole(128, 128), whole(128, 128)]
        + [whole(5, 16, 256), whole(4, 8, 128)],
        [sds(4, 60, 8, 128)],
    )(ocean_state, lo, hi, left, right, weights, top)

    side = pl.BlockSpec((136, 128), lambda *_: (0, 0))
    pair = sds(2, 128, 128)
    send_sums, res, z, y, w, v = call(
        ice_kernel,
        "ice",
        [SMEM, whole(128, 4), whole(256, 128), whole(LEAD, 4, 128), whole(LEAD, 4, 128), side, side]
        + ice_specs
        + [whole(128, 128)],
        [sds(256, 128), pair, pair, pair, pair, pair],
    )(pos, owner, got_melt, lo, hi, left[128:], right[128:], *ice, nodemap)
    got_sums = exchange(send_sums)
    velocity, residual = call(
        update_kernel,
        "update",
        [whole(256, 128)] + [whole(2, 128, 128)] * 6,
        [pair, pair],
    )(got_sums, first_guess, res, z, y, w, v)
    return (fields, melt_mean, velocity, residual)


def solution(mesh):
    split = Mesh(
        mesh.devices.reshape(mesh.shape["grp"], mesh.shape["gx"], 4, 4),
        ("grp", "gx", "gy_0", "gy_1"),
    )
    field = P(("grp", "gx"), GY)
    pair = P(None, ("grp", "gx"), GY)
    levels = P(None, None, ("grp", "gx"), GY)
    lists = P(("grp", "gx"), GY, None)
    placed = (levels, field, field, lists, lists, P(("grp", "gx"), GY, None, None))
    placed = placed + (field,) * 5 + (pair, pair)
    return jax.shard_map(
        shards,
        mesh=split,
        in_specs=placed,
        out_specs=(levels, field, pair, pair),
        check_vma=False,
    )
```

```python
import jax
import jax.numpy as jnp
from jax import lax
from jax.experimental import pallas as pl
from jax.experimental.pallas import tpu as pltpu
from jax.sharding import Mesh
from jax.sharding import PartitionSpec as P


NSUB = 4
GY = ("gy_0", "gy_1")
XAXES = ("grp", "gx")
ALL = ("grp", "gx", "gy_0", "gy_1")
LEAD = 72
DEEP = 960
SIDE_Y = 248
F32 = jnp.float32
BF16 = jnp.bfloat16
I32 = jnp.int32


def iota(shape, dim):
    return lax.broadcasted_iota(I32, shape, dim)


def split3(x):
    high = x.astype(BF16)
    rest = x - high.astype(F32)
    mid = rest.astype(BF16)
    low = (rest - mid.astype(F32)).astype(BF16)
    return high, mid, low


def onehot(hit):
    return jnp.where(hit, 1.0, 0.0).astype(BF16)


def dot_tn(a, b):
    return lax.dot_general(a, b, (((0,), (0,)), ((), ())), preferred_element_type=F32)


def dot_nt(a, b):
    return lax.dot_general(a, b, (((1,), (1,)), ((), ())), preferred_element_type=F32)


def spread(table, half, out_ref):
    row = iota((128, 128), 0) & 15
    group = iota((128, 128), 1) >> 2
    after = pltpu.roll(table, 127, 0)
    before = pltpu.roll(table, 1, 0)
    parts = []
    for dx in range(3):
        part = jnp.where((group == 3 * dx) & (row > 0), before, 0.0)
        part = jnp.where(group == 3 * dx + 1, table, part)
        part = jnp.where((group == 3 * dx + 2) & (row < 15), after, part)
        parts.append(part)
    none = jnp.zeros((16, 128), F32)
    own = parts[1] + jnp.concatenate([none, parts[0][:112]], 0)
    own = own + jnp.concatenate([parts[2][16:], none], 0)
    first = jnp.where(half == 0, parts[0][112:], 0.0)
    last = jnp.where(half == 1, parts[2][:16], 0.0)
    out_ref[pl.ds(half * 128, 128), :] = own
    out_ref[pl.ds((1 - half) * 128, 128), :] = jnp.concatenate(
        [first, jnp.zeros((96, 128), F32), last], 0
    )


def columns_of(owner_ref):
    node = owner_ref[...].astype(F32)
    return jnp.transpose(jnp.concatenate([node, node], 0)).astype(I32)


def draft_kernel(owner_ref, thick_ref, out_ref):
    lane = iota((128, 128), 1)
    parts = split3(thick_ref[...])
    node = columns_of(owner_ref)
    table = jnp.zeros((128, 128), F32)
    for s in range(4):
        column = node[:, s : s + 1]
        pick = onehot(lane == (column >> 7))
        rows = jnp.dot(pick, parts[0], preferred_element_type=F32)
        rows = rows + jnp.dot(pick, parts[1], preferred_element_type=F32)
        rows = rows + jnp.dot(pick, parts[2], preferred_element_type=F32)
        value = jnp.sum(jnp.where(lane == (column & 127), rows, 0.0), 1, keepdims=True)
        table = jnp.where((lane & 3) == s, 0.9 * value, table)
    spread(table, lax.axis_index("grp"), out_ref)


def ice_fields(refs):
    thick, visc, fric, ground, coup, drive, guess = refs
    return (
        lambda at: thick[at],
        lambda at: visc[at],
        lambda at: fric[at] * ground[at].astype(F32),
        lambda at: coup[at],
        lambda at: drive[(0,) + at],
        lambda at: drive[(1,) + at],
        lambda at: guess[(0,) + at],
        lambda at: guess[(1,) + at],
    )


WHOLE = (slice(None), slice(None))


def pack_y_kernel(
    state_ref, diff_ref, wet_ref, col_ref, slot_ref, owner_ref,
    thick, visc, fric, ground, coup, drive, guess,
    side_ref, slotmap_ref, nodemap_ref, lead_ref,
):
    col = col_ref[...]
    slot = slot_ref[...]
    hit = iota((8, 256), 0) == (col >> 7)
    peer = jnp.where(hit, ((slot >> 2) + 1).astype(F32), 0.0)
    which = jnp.where(hit, (slot & 3).astype(F32), 0.0)
    lanes = onehot(iota((128, 256), 0) == (col & 127))
    both = dot_nt(jnp.concatenate([peer, which], 0).astype(BF16), lanes)
    slotmap = jnp.where(both[:8] > 0.5, 4.0 * both[:8] + both[8:] - 3.0, 0.0)
    slotmap_ref[...] = slotmap

    node = columns_of(owner_ref)
    lane = iota((128, 128), 1)
    number = iota((128, 128), 0).astype(F32) + 1.0
    peers = []
    whichs = []
    cols = []
    for s in range(4):
        column = node[:, s : s + 1]
        hit = lane == (column >> 7)
        peers.append(jnp.where(hit, number, 0.0).astype(BF16))
        whichs.append(jnp.where(hit, float(s), 0.0).astype(BF16))
        cols.append(onehot(lane == (column & 127)))
    cols = jnp.concatenate(cols, 0)
    peer = dot_tn(jnp.concatenate(peers, 0), cols)
    which = dot_tn(jnp.concatenate(whichs, 0), cols)
    nodemap_ref[...] = jnp.where(peer > 0.5, 4.0 * peer + which - 3.0, 0.0)

    for f in range(4):
        lead_ref[8 * f : 8 * f + 8] = state_ref[480 * f : 480 * f + 8]
    lead_ref[32:40] = diff_ref[...]
    lead_ref[40:48] = wet_ref[...].astype(F32)
    lead_ref[48:56] = slotmap
    lead_ref[56:64] = jnp.zeros((8, 128), F32)

    place = iota((8, 128), 1) >> 3

    def edges(get):
        acc = jnp.zeros((8, 128), F32)
        for r in range(8):
            acc = jnp.where(place == r + 4, pltpu.roll(get(r), (8 * (r + 4) + 4) % 128, 1), acc)
        return acc

    side_ref[0:8] = edges(lambda r: lead_ref[pl.ds(r, 8, stride=8), :])

    def group(g, carry):
        at = pl.multiple_of(g * 64, 64)
        side_ref[pl.ds(pl.multiple_of(8 + 8 * g, 8), 8), :] = edges(
            lambda r: state_ref[pl.ds(at + r, 8, stride=8), :]
        )
        return carry

    lax.fori_loop(0, 30, group, 0)

    gets = ice_fields((thick, visc, fric, ground, coup, drive, guess))
    gets = gets + (lambda at: nodemap_ref[...],)
    place = lane >> 3
    acc = jnp.zeros((128, 128), F32)
    for a, get in enumerate(gets):
        acc = jnp.where(place == a, pltpu.roll(get(WHOLE), 8 * a + 4, 1), acc)
    side_ref[SIDE_Y : SIDE_Y + 128] = acc


def merged(left, right):
    return jnp.where((iota(left.shape, 1) & 4) == 0, left, right)


def pack_x_kernel(
    lead_ref, nodemap_ref, left_ref, right_ref,
    thick, visc, fric, ground, coup, drive, guess,
    up_ref, down_ref,
):
    for i in range(8):
        up_ref[4 * i : 4 * i + 4] = lead_ref[8 * i + 4 : 8 * i + 8]
        down_ref[4 * i : 4 * i + 4] = lead_ref[8 * i : 8 * i + 4]
    top = (pl.ds(0, 4), slice(None))
    end = (pl.ds(124, 4), slice(None))
    gets = ice_fields((thick, visc, fric, ground, coup, drive, guess))
    for a, get in enumerate(gets):
        up_ref[32 + 4 * a : 36 + 4 * a] = get(end)
        down_ref[32 + 4 * a : 36 + 4 * a] = get(top)
    up_ref[64:68] = nodemap_ref[124:128]
    down_ref[64:68] = nodemap_ref[0:4]
    up_ref[68:72] = merged(left_ref[SIDE_Y + 124 : SIDE_Y + 128], right_ref[SIDE_Y + 124 : SIDE_Y + 128])
    down_ref[68:72] = merged(left_ref[SIDE_Y : SIDE_Y + 4], right_ref[SIDE_Y : SIDE_Y + 4])
    side = merged(left_ref[0:8], right_ref[0:8])
    up_ref[LEAD : LEAD + 8] = side
    down_ref[LEAD : LEAD + 8] = side


def pack_deep_kernel(state_ref, left_ref, right_ref, up_ref, down_ref):
    def group(g, carry):
        at = pl.multiple_of(g * 64, 64)
        to = pl.multiple_of(g * 32, 32)
        for r in range(4):
            up_ref[pl.ds(to + r, 8, stride=4), :] = state_ref[pl.ds(at + 4 + r, 8, stride=8), :]
            down_ref[pl.ds(to + r, 8, stride=4), :] = state_ref[pl.ds(at + r, 8, stride=8), :]
        return carry

    lax.fori_loop(0, 30, group, 0)
    side = merged(left_ref[8:SIDE_Y], right_ref[8:SIDE_Y])
    up_ref[DEEP : DEEP + 240] = side
    down_ref[DEEP : DEEP + 240] = side


def whole_side(left, right, lo, hi):
    lane = iota(left.shape, 1)
    far = pltpu.roll(jnp.where(lane < 64, hi, lo), 64, 1)
    return jnp.where((lane < 32) | (lane >= 96), far, merged(left, right))


def turn(x, shift, axis):
    return pltpu.roll(x, shift % x.shape[axis], axis)


def lookup(parts, owner, lane_of):
    pick = onehot(iota((256, 128), 0) == owner)
    found = jnp.dot(parts, pick, preferred_element_type=F32)
    found = found[0:48] + found[48:96] + found[96:144]
    return jnp.sum(jnp.where(iota((48, 128), 0) == lane_of, found, 0.0), 0, keepdims=True)


def table_parts(table):
    turned = jnp.transpose(table)[0:48]
    return jnp.concatenate(split3(turned), 0)


def decode(code, half, group):
    number = code.astype(I32) - 1
    owner = jnp.where(number >= 0, half * 128 + (number >> 2), -1)
    return owner, 4 * group + (number & 3)


def pack_rows(x):
    lane = iota((16, 128), 1)
    moved = jnp.where(lane < 8, pltpu.roll(x, 4, 1), 0.0)
    moved = pltpu.roll(moved, 0, 1, stride=8, stride_axis=0)
    return jnp.sum(moved, 0, keepdims=True)


def unpack_rows(row):
    lane = iota((16, 128), 1)
    turned = [row] + [pltpu.roll(row, 128 - 8 * r, 1) for r in range(1, 16)]
    moved = jnp.where(lane < 8, jnp.concatenate(turned, 0), 0.0)
    return pltpu.roll(moved, 124, 1)


def halves():
    half = lax.axis_index("grp")
    bx = half * 8 + lax.axis_index("gx")
    return half, jnp.maximum(bx - 1, 0) >> 3, jnp.minimum(bx + 1, 15) >> 3


def top_kernel(
    lead_ref, lo_ref, hi_ref, left_ref, right_ref, table_ref,
    top_ref, melt_ref, weight_ref, send_ref, turn_ref,
):
    half, half_lo, half_hi = halves()
    side = whole_side(
        left_ref[0:8], right_ref[0:8], lo_ref[LEAD : LEAD + 8], hi_ref[LEAD : LEAD + 8]
    )
    for c in range(16):
        p = (c + 4) % 16
        turn_ref[8 * c : 8 * c + 8] = pltpu.roll(side, (128 - 8 * p - 4) % 128, 1)
    lane = iota((16, 128), 1)
    edge = (lane < 4) | (lane >= 124)

    def padded(i):
        centre = jnp.concatenate(
            [lead_ref[8 * i : 8 * i + 8], hi_ref[4 * i : 4 * i + 4], lo_ref[4 * i : 4 * i + 4]], 0
        )
        edges = jnp.where(edge, turn_ref[pl.ds(i, 16, stride=8), :], 0.0)
        return jnp.concatenate([centre, edges], 1)

    fields = [padded(f) for f in range(4)]
    diff = padded(4)
    wet = padded(5)
    code = padded(6)
    weights = []
    for axis, shift in ((0, -1), (0, 1), (1, -1), (1, 1)):
        weights.append(0.5 * (diff + turn(diff, shift, axis)) * wet * turn(wet, shift, axis))
    keep = 1.0 - (weights[0] + weights[1] + weights[2] + weights[3])
    for j, w in enumerate(weights + [keep]):
        centre = w[:, 0:128]
        weight_ref[16 * j : 16 * j + 12] = jnp.concatenate([w[12:16, 0:128], w[0:8, 0:128]], 0)
        weight_ref[16 * j + 12 : 16 * j + 16] = w[8:12, 0:128]
        east = jnp.where(lane < 4, pltpu.roll(centre, 4, 1), pltpu.roll(w[:, 128:256], 4, 1))
        west = jnp.where(lane < 4, pltpu.roll(w[:, 128:256], 4, 1), pltpu.roll(centre, 4, 1))
        for k, strip in enumerate((east, west)):
            strip = jnp.where(lane < 8, strip, 0.0)
            strip = jnp.sum(pltpu.roll(strip, 0, 1, stride=8, stride_axis=0), 0, keepdims=True)
            weight_ref[80 + 2 * j + k : 81 + 2 * j + k] = pltpu.roll(strip, 32, 1)
    weight_ref[90:96] = jnp.zeros((6, 128), F32)

    row = iota((16, 128), 0)
    half_at = jnp.where(row < 8, half, jnp.where(row < 12, half_hi, half_lo))
    dx = jnp.where(row < 8, 1, jnp.where(row < 12, 2, 0))
    owner, lane_of = decode(code[:, 0:128], half_at, 3 * dx + 1)
    flat = iota((1, 128), 1)
    place = flat >> 3
    half_at = jnp.where(place < 4, half_lo, jnp.where(place < 12, half, half_hi))
    dx = jnp.where(place < 4, 0, jnp.where(place < 12, 1, 2))
    dy = jnp.where((flat & 4) == 0, 0, 2)
    side_owner, side_lane = decode(side[6:7], half_at, 3 * dx + dy)
    parts = table_parts(table_ref[...])
    none = jnp.zeros((1, 128), F32)
    found = [
        none if r in (11, 12) else lookup(parts, owner[r : r + 1], lane_of[r : r + 1]) for r in range(16)
    ]
    side_found = lookup(parts, side_owner, side_lane)
    turned = []
    for c in range(16):
        p = (c + 4) % 16
        turned.append(pltpu.roll(side_found, (128 - 8 * p - 4) % 128, 1))
    edges = jnp.where(edge, jnp.concatenate(turned, 0), 0.0)
    draft = jnp.concatenate([jnp.concatenate(found, 0), edges], 1)
    cover = jnp.where(code > 0.5, 1.0, 0.0)

    total = jnp.zeros((8, 128), F32)
    for _ in range(NSUB):
        temp, salt, east, north = fields
        speed = jnp.sqrt(east * east + north * north + 0.01)
        freezing = -0.5 * salt + 0.3 * draft - 0.2
        melt = 0.5 * cover * (temp - freezing) * speed
        drag = 0.05 * cover * speed
        total = total + melt[0:8, 0:128]
        loss = (0.3 * melt, 0.2 * melt, drag * east, drag * north)
        changed = []
        for f in range(4):
            x = fields[f]
            flux = weights[0] * (turn(x, -1, 0) - x) + weights[1] * (turn(x, 1, 0) - x)
            flux = flux + weights[2] * (turn(x, -1, 1) - x) + weights[3] * (turn(x, 1, 1) - x)
            changed.append(x + flux - loss[f])
        fields = changed
    for f in range(4):
        top_ref[8 * f : 8 * f + 8] = fields[f][0:8, 0:128]
    mean = total * (1.0 / NSUB)
    melt_ref[...] = mean

    number = lead_ref[48:56].astype(I32) - 1
    peers = []
    values = []
    for r in range(8):
        at = number[r : r + 1]
        peers.append(onehot(iota((128, 128), 0) == (at >> 2)))
        values.append(jnp.where((iota((128, 128), 0) & 3) == (at & 3), mean[r : r + 1], 0.0))
    peers = jnp.concatenate(peers, 1)
    values = jnp.concatenate(split3(jnp.concatenate(values, 1)), 0)
    table = dot_nt(peers, values)
    spread(table[:, 0:128] + table[:, 128:256] + table[:, 256:384], half, send_ref)


def bulk_kernel(
    state_ref, lo_ref, hi_ref, left_ref, right_ref, weight_ref, top_ref, out_ref, wide_ref,
):
    lane = iota((8, 128), 1)
    outer = (lane & 4) == 0

    for k in range(90):
        wide_ref[8 * k : 8 * k + 8] = jnp.broadcast_to(weight_ref[k : k + 1], (8, 128))

    def weight(k):
        return wide_ref[8 * k : 8 * k + 8]

    def group(g, carry):
        at = pl.multiple_of(g * 64, 64)
        far = pl.multiple_of(g * 32, 32)
        side = pl.multiple_of(8 * g, 8)
        x = [lo_ref[pl.ds(far + r, 8, stride=4), :] for r in range(4)]
        x = x + [state_ref[pl.ds(at + r, 8, stride=8), :] for r in range(8)]
        x = x + [hi_ref[pl.ds(far + r, 8, stride=4), :] for r in range(4)]
        own = jnp.zeros((8, 128), F32)
        for p in range(16):
            own = jnp.where((lane >> 3) == p, pltpu.roll(x[p], (8 * p + 4) % 128, 1), own)
        near = whole_side(
            left_ref[pl.ds(pl.multiple_of(side + 8, 8), 8), :],
            right_ref[pl.ds(pl.multiple_of(side + 8, 8), 8), :],
            lo_ref[pl.ds(pl.multiple_of(side + DEEP, 8), 8), :],
            hi_ref[pl.ds(pl.multiple_of(side + DEEP, 8), 8), :],
        )
        strips = [jnp.where(outer, own, near), jnp.where(outer, near, own)]
        for substep in range(NSUB):
            ends = jnp.where((lane & 7) == 4, strips[0], strips[1])
            new = [None] * 16
            for p in range(substep + 1, 15 - substep):
                end = pltpu.roll(ends, (128 - 8 * p - 4) % 128, 1)
                here = x[p]
                after = pltpu.roll(jnp.where(lane == 0, end, here), 127, 1)
                before = pltpu.roll(jnp.where(lane == 127, end, here), 1, 1)
                y = weight(64 + p) * here + weight(p) * x[p + 1] + weight(16 + p) * x[p - 1]
                new[p] = y + weight(32 + p) * after + weight(48 + p) * before
            if substep + 1 < NSUB:
                moved = []
                for k in range(2):
                    s = strips[k]
                    y = weight(88 + k) * s + weight(80 + k) * pltpu.roll(s, 120, 1)
                    y = y + weight(82 + k) * pltpu.roll(s, 8, 1)
                    moved.append(y + weight(84 + k) * pltpu.roll(s, 127, 1) + weight(86 + k) * pltpu.roll(s, 1, 1))
                strips = moved
            x = new
        for r in range(8):
            out_ref[pl.ds(at + r, 8, stride=8), :] = x[r + 4]
        return carry

    lax.fori_loop(0, 30, group, 0, unroll=2)
    for f in range(4):
        out_ref[480 * f : 480 * f + 8] = top_ref[8 * f : 8 * f + 8]


def two_sum(a, b):
    s = a + b
    t = s - a
    return s, (a - (s - t)) + (b - t)


def two_product(a, b):
    def split(v):
        c = 4097.0 * v
        high = c - (c - v)
        return high, v - high

    p = a * b
    a1, a2 = split(a)
    b1, b2 = split(b)
    return p, ((a1 * b1 - p) + a1 * b2 + a2 * b1) + a2 * b2


def add_pair(a, b):
    s, e = two_sum(a[0], b[0])
    e = e + (a[1] + b[1])
    return two_sum(s, e)


def less_scaled(a, k, b):
    p, e = two_product(k, b[0])
    return add_pair(a, (-p, -(e + k * b[1])))


def fold(pair, axis, sizes):
    for size in sizes:
        turned = tuple(pltpu.roll(v, size, axis) for v in pair)
        pair = add_pair(pair, turned)
    return pair


def tiles_sum(x, low=None):
    total = x[0:8]
    error = jnp.zeros((8, 128), F32) if low is None else low[0:8]
    for r in range(8, x.shape[0], 8):
        total, e = two_sum(total, x[r : r + 8])
        error = error + e
        if low is not None:
            error = error + low[r : r + 8]
    return fold(two_sum(total, error), 0, (4, 2, 1))


def ice_kernel(
    owner_ref, table_ref, lo_ref, hi_ref, left_ref, right_ref,
    thick, visc, fric, ground, coup, drive, guess, nodemap_ref,
    send_ref, res_ref, z_ref, y_ref, w_ref, v_ref,
):
    half, half_lo, half_hi = halves()
    side = merged(left_ref[SIDE_Y : SIDE_Y + 128], right_ref[SIDE_Y : SIDE_Y + 128])
    side = jnp.concatenate([side, hi_ref[68:72], lo_ref[68:72]], 0)
    gets = ice_fields((thick, visc, fric, ground, coup, drive, guess))
    gets = gets + (lambda at: nodemap_ref[...],)
    lane = iota((136, 128), 1)
    edge = (lane < 4) | (lane >= 124)

    def padded(a):
        at = 32 + 4 * a
        centre = jnp.concatenate([gets[a](WHOLE), hi_ref[at : at + 4], lo_ref[at : at + 4]], 0)
        edges = jnp.where(edge, pltpu.roll(side, (128 - 8 * a - 4) % 128, 1), 0.0)
        return jnp.concatenate([centre, edges], 1)

    table = table_ref[...]
    mine = table_ref[pl.ds(pl.multiple_of(half * 128, 128), 128), :]
    node = columns_of(owner_ref)
    lane = iota((128, 128), 1)
    rows = []
    cols = []
    for s in range(4):
        column = node[:, s : s + 1]
        rows.append(onehot(lane == (column >> 7)))
        cols.append(jnp.where(lane == (column & 127), mine[:, 16 + s : 17 + s], 0.0))
    cols = jnp.concatenate(split3(jnp.concatenate(cols, 0)), 1)
    melt = dot_tn(jnp.concatenate(rows, 0), cols)
    melt = melt[:, 0:128] + melt[:, 128:256] + melt[:, 256:384]

    code = padded(8)
    row = iota((136, 256), 0)
    col = iota((136, 256), 1)
    half_at = jnp.where(row < 128, half, jnp.where(row < 132, half_hi, half_lo))
    dx = jnp.where(row < 128, 1, jnp.where(row < 132, 2, 0))
    dy = jnp.where(col < 128, 1, jnp.where(col < 192, 2, 0))
    owner, lane_of = decode(code, half_at, 3 * dx + dy)
    parts = table_parts(table)
    rim = [
        lookup(parts, owner[r : r + 1, :128], lane_of[r : r + 1, :128]) for r in range(128, 136)
    ]
    side_owner = (owner[:, 128:] + 1).astype(F32)
    side_lane = lane_of[:, 128:].astype(F32)
    spare = jnp.zeros((8, 128), F32)
    sides = []
    for block in range(9):
        if block < 8:
            piece_owner = side_owner[16 * block : 16 * block + 16]
            piece_lane = side_lane[16 * block : 16 * block + 16]
        else:
            piece_owner = jnp.concatenate([side_owner[128:136], spare], 0)
            piece_lane = jnp.concatenate([side_lane[128:136], spare], 0)
        at_owner = pack_rows(piece_owner).astype(I32) - 1
        at_lane = pack_rows(piece_lane).astype(I32)
        piece = unpack_rows(lookup(parts, at_owner, at_lane))
        sides.append(piece if block < 8 else piece[0:8])
    melt = jnp.concatenate([melt] + rim, 0)
    melt = jnp.concatenate([melt, jnp.concatenate(sides, 0)], 1)

    thickness = padded(0)
    inside = thickness > 0.0
    thinned = thickness * jnp.exp(-0.3 * melt)
    depth = padded(1) * thinned
    base = padded(2) + 0.2
    cross = 0.9 * base * padded(3)
    w_e = 0.5 * (depth + turn(depth, -1, 0))
    w_w = 0.5 * (depth + turn(depth, 1, 0))
    w_n = 0.5 * (depth + turn(depth, -1, 1))
    w_s = 0.5 * (depth + turn(depth, 1, 1))
    diagonal = w_e + w_w + w_n + w_s + base
    inverse = jnp.where(inside, 1.0 / diagonal, 0.0)

    def apply(pair):
        out = []
        for a in range(2):
            x = pair[a]
            beside = w_e * turn(x, -1, 0) + w_w * turn(x, 1, 0)
            beside = beside + w_n * turn(x, -1, 1) + w_s * turn(x, 1, 1)
            out.append(diagonal * x - beside + cross * pair[1 - a])
        return out

    first = [padded(6), padded(7)]
    image = apply(first)
    res = [padded(4 + a) * thinned - image[a] for a in range(2)]
    z = [res[a] * inverse for a in range(2)]
    y = apply(z)
    w = [y[a] * inverse for a in range(2)]
    v = apply(w)
    inner = (slice(0, 128), slice(0, 128))
    lane = iota((256, 128), 1)
    message = jnp.zeros((256, 128), F32)
    for k, (one, two) in enumerate(((res, z), (z, y), (y, w), (w, v))):
        product = jnp.concatenate([one[a][inner] * two[a][inner] for a in range(2)], 0)
        pair = fold(tiles_sum(product), 1, (64, 32, 16, 8, 4, 2, 1))
        message = jnp.where(lane == k, pair[0][0:1], message)
        message = jnp.where(lane == k + 4, pair[1][0:1], message)
    send_ref[...] = message
    for a in range(2):
        res_ref[a] = res[a][inner]
        z_ref[a] = z[a][inner]
        y_ref[a] = y[a][inner]
        w_ref[a] = w[a][inner]
        v_ref[a] = v[a][inner]


def update_kernel(sum_ref, guess_ref, res_ref, z_ref, y_ref, w_ref, v_ref, vel_ref, left_ref):
    got = sum_ref[...]
    pair = tiles_sum(got, pltpu.roll(got, 124, 1))
    norm, curve, mixed, far = ((pair[0][0:1, k : k + 1], pair[1][0:1, k : k + 1]) for k in range(4))
    step = norm[0] / curve[0]
    rest = less_scaled(norm, step, curve)
    along = less_scaled(curve, step, mixed)
    norm_next = (rest[0] - step * along[0]) + (rest[1] - step * along[1])
    ratio = norm_next / norm[0]
    curve_next = less_scaled(along, step, less_scaled(mixed, step, far))[0]
    curve_next = curve_next + 2.0 * ratio * along[0] + ratio * ratio * curve[0]
    step_next = norm_next / curve_next
    one = step + step_next * (1.0 + ratio)
    two = step_next * step
    for a in range(2):
        vel_ref[a] = guess_ref[a] + one * z_ref[a] - two * w_ref[a]
        left_ref[a] = res_ref[a] - one * y_ref[a] + two * v_ref[a]


def sds(*shape):
    return jax.ShapeDtypeStruct(shape, F32)


SMALL = 24 << 20


def near(*shape):
    return pltpu.VMEM(shape, F32)


def call(kernel, outs, *args, stay=(), limit=None, **kw):
    args = [x if any(x is y for y in stay) else here(x) for x in args]
    vmem = pl.BlockSpec(memory_space=pltpu.VMEM)
    return pl.pallas_call(
        kernel,
        in_specs=[vmem] * len(args),
        out_specs=[vmem] * len(outs),
        out_shape=outs,
        compiler_params=pltpu.CompilerParams(vmem_limit_bytes=limit),
        **kw,
    )(*args)


def here(x):
    return pltpu.with_memory_space_constraint(x, pltpu.VMEM)


def swap(up, down, axes):
    size = lax.axis_size(axes)
    forward = [(i, i + 1) for i in range(size - 1)]
    low = lax.ppermute(up, axes, forward)
    high = lax.ppermute(down, axes, [(b, a) for a, b in forward])
    return here(low), here(high)


def exchange(table):
    return here(lax.all_to_all(table, ALL, split_axis=0, concat_axis=0, tiled=True))


def shards(
    ocean_state, diffusivity, wet_mask, coast_column, coast_slot, owner_node,
    thickness, viscosity, friction, grounded, coupling, driving, first_guess,
):
    owner = owner_node[0, 0].T
    columns = coast_column.reshape(1, 256)
    slots = coast_slot.reshape(1, 256)
    ice = (thickness, viscosity, friction, grounded, coupling, driving, first_guess)
    state = ocean_state.reshape(1920, 128)
    given = (state, diffusivity, wet_mask, columns, slots, owner) + ice

    side, _, nodemap, lead = call(
        pack_y_kernel,
        [sds(SIDE_Y + 128, 128), near(8, 128), near(128, 128), near(64, 128)],
        state, diffusivity, wet_mask, columns, slots, owner, *ice,
        stay=given,
    )
    left, right = swap(side, side, GY)
    (send_draft,) = call(draft_kernel, [sds(256, 128)], owner, thickness, stay=given, limit=SMALL)
    up, down = call(
        pack_x_kernel,
        [sds(LEAD + 8, 128), sds(LEAD + 8, 128)],
        lead, nodemap, left, right, *ice,
        stay=given,
        limit=SMALL,
    )
    lo, hi = swap(up, down, XAXES)
    up, down = call(
        pack_deep_kernel,
        [sds(DEEP + 240, 128), sds(DEEP + 240, 128)],
        state, left, right,
        stay=given,
        limit=SMALL,
    )
    deep_lo, deep_hi = swap(up, down, XAXES)
    got_draft = exchange(send_draft)

    top, melt_mean, weights, send_melt = call(
        top_kernel,
        [sds(32, 128), sds(8, 128), sds(96, 128), sds(256, 128)],
        lead, lo, hi, left, right, got_draft,
        scratch_shapes=[pltpu.VMEM((128, 128), F32)],
        limit=SMALL,
    )
    got_melt = exchange(send_melt)
    (fields,) = call(
        bulk_kernel,
        [sds(1920, 128)],
        state, deep_lo, deep_hi, left, right, weights, top,
        stay=given + (weights, top),
        limit=SMALL,
        scratch_shapes=[pltpu.VMEM((720, 128), F32)],
    )

    pair = sds(2, 128, 128)
    send_sums, res, z, y, w, v = call(
        ice_kernel,
        [sds(256, 128), pair, pair, pair, pair, pair],
        owner, got_melt, lo, hi, left, right, *ice, nodemap,
    )
    got_sums = exchange(send_sums)
    pair = sds(2, 128, 128)
    velocity, residual = call(
        update_kernel, [pair, pair], got_sums, first_guess, res, z, y, w, v,
        stay=(first_guess, res, z, y, w, v), limit=SMALL,
    )
    return (fields.reshape(ocean_state.shape), melt_mean, velocity, residual)


def solution(mesh):
    split = Mesh(
        mesh.devices.reshape(mesh.shape["grp"], mesh.shape["gx"], 4, 4),
        ("grp", "gx", "gy_0", "gy_1"),
    )
    field = P(("grp", "gx"), GY)
    pair = P(None, ("grp", "gx"), GY)
    levels = P(None, None, ("grp", "gx"), GY)
    lists = P(("grp", "gx"), GY, None)
    placed = (levels, field, field, lists, lists, P(("grp", "gx"), GY, None, None))
    placed = placed + (field,) * 5 + (pair, pair)
    return jax.shard_map(
        shards,
        mesh=split,
        in_specs=placed,
        out_specs=(levels, field, pair, pair),
        check_vma=False,
    )
```

```python
import jax
import jax.numpy as jnp
from jax import lax
from jax.experimental import pallas as pl
from jax.experimental.pallas import tpu as pltpu
from jax.sharding import Mesh
from jax.sharding import PartitionSpec as P


NSUB = 4
GY = ("gy_0", "gy_1")
XAXES = ("grp", "gx")
ALL = ("grp", "gx", "gy_0", "gy_1")
LEAD = 24
DEEP = 960
SIDE_Y = 240
F32 = jnp.float32
BF16 = jnp.bfloat16
I32 = jnp.int32


def iota(shape, dim):
    return lax.broadcasted_iota(I32, shape, dim)


def split3(x):
    high = x.astype(BF16)
    rest = x - high.astype(F32)
    mid = rest.astype(BF16)
    low = (rest - mid.astype(F32)).astype(BF16)
    return high, mid, low


def onehot(hit):
    return jnp.where(hit, 1.0, 0.0).astype(BF16)


def dot_tn(a, b):
    return lax.dot_general(a, b, (((0,), (0,)), ((), ())), preferred_element_type=F32)


def dot_nt(a, b):
    return lax.dot_general(a, b, (((1,), (1,)), ((), ())), preferred_element_type=F32)


def spread(table, half, out_ref, stride):
    row = iota((128, 128), 0) & 15
    group = iota((128, 128), 1) >> 2
    after = pltpu.roll(table, 127, 0)
    before = pltpu.roll(table, 1, 0)
    parts = []
    for dx in range(3):
        part = jnp.where((group == 3 * dx) & (row > 0), before, 0.0)
        part = jnp.where(group == 3 * dx + 1, table, part)
        part = jnp.where((group == 3 * dx + 2) & (row < 15), after, part)
        parts.append(part)
    none = jnp.zeros((16, 128), F32)
    own = parts[1] + jnp.concatenate([none, parts[0][:112]], 0)
    own = own + jnp.concatenate([parts[2][16:], none], 0)
    first = jnp.where(half == 0, parts[0][112:], 0.0)
    last = jnp.where(half == 1, parts[2][:16], 0.0)
    other = jnp.concatenate([first, jnp.zeros((96, 128), F32), last], 0)
    size = 128 * stride
    if stride > 1:
        out_ref[...] = jnp.zeros(out_ref.shape, F32)
    out_ref[pl.ds(pl.multiple_of(half * size, size), 128, stride=stride), :] = own
    out_ref[pl.ds(pl.multiple_of((1 - half) * size, size), 128, stride=stride), :] = other


def place_of():
    half = lax.axis_index("grp")
    bx = half * 8 + lax.axis_index("gx")
    by = lax.axis_index("gy_0") * 4 + lax.axis_index("gy_1")
    return half, bx, by


def first_of(near, far):
    return jnp.where((iota(near.shape, 1) & 4) == 0, near, pltpu.roll(far, 4, 1))


def last_of(near, far):
    return jnp.where((iota(near.shape, 1) & 4) == 0, pltpu.roll(near, 124, 1), far)


def columns_of(owner_ref):
    node = owner_ref[...].astype(F32)
    return jnp.transpose(jnp.concatenate([node, node], 0)).astype(I32)


def draft_kernel(owner_ref, thick_ref, state_ref, diff_ref, wet_ref, col_ref, slot_ref, out_ref, lead_ref):
    half, bx, by = place_of()
    lane = iota((128, 128), 1)
    parts = split3(thick_ref[...])
    node = columns_of(owner_ref)
    table = jnp.zeros((128, 128), F32)
    for s in range(4):
        column = node[:, s : s + 1]
        pick = onehot(lane == (column >> 7))
        rows = jnp.dot(pick, parts[0], preferred_element_type=F32)
        rows = rows + jnp.dot(pick, parts[1], preferred_element_type=F32)
        rows = rows + jnp.dot(pick, parts[2], preferred_element_type=F32)
        value = jnp.sum(jnp.where(lane == (column & 127), rows, 0.0), 1, keepdims=True)
        table = jnp.where((lane & 3) == s, 0.9 * value, table)
    spread(table, half, out_ref, 2)

    col = col_ref[...]
    slot = slot_ref[...]
    hit = iota((8, 256), 0) == (col >> 7)
    peer = jnp.where(hit, ((slot >> 2) + 1).astype(F32), 0.0)
    which = jnp.where(hit, (slot & 3).astype(F32), 0.0)
    lanes = onehot(iota((128, 256), 0) == (col & 127))
    both = dot_nt(jnp.concatenate([peer, which], 0).astype(BF16), lanes)
    for f in range(4):
        lead_ref[8 * f : 8 * f + 8] = state_ref[f, 0]
    lead_ref[32:40] = jnp.where(wet_ref[...] > 0, diff_ref[...], 0.0)
    lead_ref[40:48] = jnp.where(both[:8] > 0.5, 4.0 * both[:8] + both[8:] - 3.0, 0.0)
    lead_ref[48:64] = jnp.zeros((16, 128), F32)
    side = edges(lambda r: lead_ref[pl.ds(r, 8, stride=8), :])
    flat = iota((1, 128), 1)
    for dy, join in ((1, first_of), (-1, last_of)):
        pairs = [join(side[2 * j : 2 * j + 1], side[2 * j + 1 : 2 * j + 2]) for j in range(3)]
        one = jnp.where(flat >= 64, pltpu.roll(pairs[2], 32, 1), 0.0)
        two = jnp.where(flat < 64, pltpu.roll(pairs[0], 96, 1), pltpu.roll(pairs[1], 32, 1))
        for dx in (-1, 0, 1):
            to_x = bx + dx
            to_y = by + dy

            @pl.when((to_x >= 0) & (to_x < 16) & (to_y >= 0) & (to_y < 16))
            def _():
                at = 2 * (to_x * 16 + to_y)
                out_ref[pl.ds(at, 1), :] = out_ref[pl.ds(at, 1), :] + one
                out_ref[pl.ds(at + 1, 1), :] = two


def edges(get):
    place = iota((8, 128), 1) >> 3
    acc = jnp.zeros((8, 128), F32)
    for r in range(8):
        acc = jnp.where(place == r + 4, pltpu.roll(get(r), (8 * (r + 4) + 4) % 128, 1), acc)
    return acc


def ice_fields(refs):
    thick, visc, fric, ground, coup, drive, guess = refs
    return (
        lambda at: thick[at],
        lambda at: visc[at],
        lambda at: fric[at] * ground[at].astype(F32),
        lambda at: coup[at],
        lambda at: drive[(0,) + at],
        lambda at: drive[(1,) + at],
        lambda at: guess[(0,) + at],
        lambda at: guess[(1,) + at],
    )


WHOLE = (slice(None), slice(None))


def pack_y_kernel(
    state_ref, nodemap_ref,
    thick, visc, fric, ground, coup, drive, guess,
    side_ref,
):
    def group(g, carry):
        at = pl.multiple_of(g * 64, 64)
        side_ref[pl.ds(pl.multiple_of(8 * g, 8), 8), :] = edges(
            lambda r: state_ref[pl.ds(at + r, 8, stride=8), :]
        )
        return carry

    lax.fori_loop(0, 30, group, 0, unroll=2)

    gets = ice_fields((thick, visc, fric, ground, coup, drive, guess))
    gets = gets + (lambda at: nodemap_ref[...],)
    place = iota((128, 128), 1) >> 3
    acc = jnp.zeros((128, 128), F32)
    for a, get in enumerate(gets):
        acc = jnp.where(place == a, pltpu.roll(get(WHOLE), 8 * a + 4, 1), acc)
    side_ref[SIDE_Y : SIDE_Y + 128] = acc


def merged(left, right):
    return jnp.where((iota(left.shape, 1) & 4) == 0, left, right)


def pack_x_kernel(
    lead_ref, owner_ref,
    thick, visc, fric, ground, coup, drive, guess,
    up_ref, down_ref, nodemap_ref,
):
    node = columns_of(owner_ref)
    lane = iota((128, 128), 1)
    number = iota((128, 128), 0).astype(F32) + 1.0
    peers = []
    whichs = []
    cols = []
    for s in range(4):
        column = node[:, s : s + 1]
        hit = lane == (column >> 7)
        peers.append(jnp.where(hit, number, 0.0).astype(BF16))
        whichs.append(jnp.where(hit, float(s), 0.0).astype(BF16))
        cols.append(onehot(lane == (column & 127)))
    cols = jnp.concatenate(cols, 0)
    peer = dot_tn(jnp.concatenate(peers, 0), cols)
    which = dot_tn(jnp.concatenate(whichs, 0), cols)
    nodemap_ref[...] = jnp.where(peer > 0.5, 4.0 * peer + which - 3.0, 0.0)

    for i in range(6):
        up_ref[4 * i : 4 * i + 4] = lead_ref[8 * i + 4 : 8 * i + 8]
        down_ref[4 * i : 4 * i + 4] = lead_ref[8 * i : 8 * i + 4]
    top = (pl.ds(0, 4), slice(None))
    end = (pl.ds(124, 4), slice(None))
    gets = ice_fields((thick, visc, fric, ground, coup, drive, guess))
    gets = gets + (lambda at: nodemap_ref[at],)
    for a, get in enumerate(gets):
        up_ref[LEAD + 4 * a : LEAD + 4 * a + 4] = get(end)
        down_ref[LEAD + 4 * a : LEAD + 4 * a + 4] = get(top)
    up_ref[60:64] = jnp.zeros((4, 128), F32)
    down_ref[60:64] = jnp.zeros((4, 128), F32)


def pack_deep_kernel(state_ref, left_ref, right_ref, up_ref, down_ref):
    def group(g, carry):
        at = pl.multiple_of(g * 64, 64)
        to = pl.multiple_of(g * 32, 32)
        for r in range(4):
            up_ref[pl.ds(to + r, 8, stride=4), :] = state_ref[pl.ds(at + 4 + r, 8, stride=8), :]
            down_ref[pl.ds(to + r, 8, stride=4), :] = state_ref[pl.ds(at + r, 8, stride=8), :]
        return carry

    lax.fori_loop(0, 30, group, 0, unroll=2)
    side = merged(left_ref[0:SIDE_Y], right_ref[0:SIDE_Y])
    up_ref[DEEP : DEEP + 240] = side
    down_ref[DEEP : DEEP + 240] = side


def whole_side(own, lo, hi):
    lane = iota(own.shape, 1)
    far = pltpu.roll(jnp.where(lane < 64, hi, lo), 64, 1)
    return jnp.where((lane < 32) | (lane >= 96), far, own)


def turn(x, shift, axis):
    return pltpu.roll(x, shift % x.shape[axis], axis)


def lookup(parts, owner, lane_of):
    pick = onehot(iota((256, 128), 0) == owner)
    found = jnp.dot(parts, pick, preferred_element_type=F32)
    found = found[0:48] + found[48:96] + found[96:144]
    return jnp.sum(jnp.where(iota((48, 128), 0) == lane_of, found, 0.0), 0, keepdims=True)


def table_parts(table):
    turned = jnp.transpose(table)[0:48]
    return jnp.concatenate(split3(turned), 0)


def decode(code, half, group):
    number = code.astype(I32) - 1
    owner = jnp.where(number >= 0, half * 128 + (number >> 2), -1)
    return owner, 4 * group + (number & 3)


def pack_rows(x):
    lane = iota((16, 128), 1)
    moved = jnp.where(lane < 8, pltpu.roll(x, 4, 1), 0.0)
    moved = pltpu.roll(moved, 0, 1, stride=8, stride_axis=0)
    return jnp.sum(moved, 0, keepdims=True)


def unpack_rows(row):
    lane = iota((16, 128), 1)
    turned = [row] + [pltpu.roll(row, 128 - 8 * r, 1) for r in range(1, 16)]
    moved = jnp.where(lane < 8, jnp.concatenate(turned, 0), 0.0)
    return pltpu.roll(moved, 124, 1)


def halves():
    half = lax.axis_index("grp")
    bx = half * 8 + lax.axis_index("gx")
    return half, jnp.maximum(bx - 1, 0) >> 3, jnp.minimum(bx + 1, 15) >> 3


def top_kernel(
    lead_ref, lo_ref, hi_ref, table_ref, ice_ref,
    top_ref, melt_ref, weight_ref, send_ref, turn_ref,
):
    half, half_lo, half_hi = halves()
    _, bx, by = place_of()
    flat = iota((1, 128), 1)

    def pairs_from(x, y):
        ok = (x >= 0) & (x < 16) & (y >= 0) & (y < 16)
        at = jnp.where(ok, 2 * (x * 16 + y), 0)
        one = table_ref[pl.ds(at, 1), :]
        two = table_ref[pl.ds(at + 1, 1), :]
        found = (pltpu.roll(two, 32, 1), pltpu.roll(two, 96, 1), pltpu.roll(one, 96, 1))
        return [jnp.where(ok & (flat >= 32) & (flat < 96), f, 0.0) for f in found]

    def columns_at(x):
        from_left = pairs_from(x, by - 1)
        from_right = pairs_from(x, by + 1)
        rows = []
        for j in range(3):
            rows.append(merged(from_left[j], pltpu.roll(from_right[j], 4, 1)))
            rows.append(merged(pltpu.roll(from_left[j], 124, 1), from_right[j]))
        return jnp.concatenate(rows + [jnp.zeros((2, 128), F32)], 0)

    side = whole_side(columns_at(bx), columns_at(bx - 1), columns_at(bx + 1))
    for c in range(16):
        p = (c + 4) % 16
        turn_ref[8 * c : 8 * c + 8] = pltpu.roll(side, (128 - 8 * p - 4) % 128, 1)
    lane = iota((16, 128), 1)
    edge = (lane < 4) | (lane >= 124)

    def padded(i):
        centre = jnp.concatenate(
            [lead_ref[8 * i : 8 * i + 8], hi_ref[4 * i : 4 * i + 4], lo_ref[4 * i : 4 * i + 4]], 0
        )
        edges = jnp.where(edge, turn_ref[pl.ds(i, 16, stride=8), :], 0.0)
        return jnp.concatenate([centre, edges], 1)

    fields = [padded(f) for f in range(4)]
    diff = padded(4)
    code = padded(5)
    weights = []
    for axis, shift in ((0, -1), (0, 1), (1, -1), (1, 1)):
        other = turn(diff, shift, axis)
        weights.append(jnp.where((diff > 0.0) & (other > 0.0), 0.5 * (diff + other), 0.0))
    keep = 1.0 - (weights[0] + weights[1] + weights[2] + weights[3])
    for j, w in enumerate(weights + [keep]):
        centre = w[:, 0:128]
        weight_ref[16 * j : 16 * j + 12] = jnp.concatenate([w[12:16, 0:128], w[0:8, 0:128]], 0)
        weight_ref[16 * j + 12 : 16 * j + 16] = w[8:12, 0:128]
        east = jnp.where(lane < 4, pltpu.roll(centre, 4, 1), pltpu.roll(w[:, 128:256], 4, 1))
        west = jnp.where(lane < 4, pltpu.roll(w[:, 128:256], 4, 1), pltpu.roll(centre, 4, 1))
        for k, strip in enumerate((east, west)):
            strip = jnp.where(lane < 8, strip, 0.0)
            strip = jnp.sum(pltpu.roll(strip, 0, 1, stride=8, stride_axis=0), 0, keepdims=True)
            weight_ref[80 + 2 * j + k : 81 + 2 * j + k] = pltpu.roll(strip, 32, 1)
    weight_ref[90:96] = jnp.zeros((6, 128), F32)

    row = iota((16, 128), 0)
    half_at = jnp.where(row < 8, half, jnp.where(row < 12, half_hi, half_lo))
    dx = jnp.where(row < 8, 1, jnp.where(row < 12, 2, 0))
    owner, lane_of = decode(code[:, 0:128], half_at, 3 * dx + 1)
    place = flat >> 3
    half_at = jnp.where(place < 4, half_lo, jnp.where(place < 12, half, half_hi))
    dx = jnp.where(place < 4, 0, jnp.where(place < 12, 1, 2))
    dy = jnp.where((flat & 4) == 0, 0, 2)
    side_owner, side_lane = decode(side[5:6], half_at, 3 * dx + dy)
    parts = table_parts(table_ref[pl.ds(0, 256, stride=2), :])
    none = jnp.zeros((1, 128), F32)
    found = [
        none if r in (11, 12) else lookup(parts, owner[r : r + 1], lane_of[r : r + 1]) for r in range(16)
    ]
    side_found = lookup(parts, side_owner, side_lane)
    turned = []
    for c in range(16):
        p = (c + 4) % 16
        turned.append(pltpu.roll(side_found, (128 - 8 * p - 4) % 128, 1))
    edges = jnp.where(edge, jnp.concatenate(turned, 0), 0.0)
    draft = jnp.concatenate([jnp.concatenate(found, 0), edges], 1)
    cover = jnp.where(code > 0.5, 1.0, 0.0)

    total = jnp.zeros((8, 128), F32)
    for _ in range(NSUB):
        temp, salt, east, north = fields
        speed = jnp.sqrt(east * east + north * north + 0.01)
        freezing = -0.5 * salt + 0.3 * draft - 0.2
        melt = 0.5 * cover * (temp - freezing) * speed
        drag = 0.05 * cover * speed
        total = total + melt[0:8, 0:128]
        loss = (0.3 * melt, 0.2 * melt, drag * east, drag * north)
        changed = []
        for f in range(4):
            x = fields[f]
            flux = weights[0] * (turn(x, -1, 0) - x) + weights[1] * (turn(x, 1, 0) - x)
            flux = flux + weights[2] * (turn(x, -1, 1) - x) + weights[3] * (turn(x, 1, 1) - x)
            changed.append(x + flux - loss[f])
        fields = changed
    for f in range(4):
        top_ref[8 * f : 8 * f + 8] = fields[f][0:8, 0:128]
    mean = total * (1.0 / NSUB)
    melt_ref[...] = mean

    number = lead_ref[40:48].astype(I32) - 1
    peers = []
    values = []
    for r in range(8):
        at = number[r : r + 1]
        peers.append(onehot(iota((128, 128), 0) == (at >> 2)))
        values.append(jnp.where((iota((128, 128), 0) & 3) == (at & 3), mean[r : r + 1], 0.0))
    peers = jnp.concatenate(peers, 1)
    values = jnp.concatenate(split3(jnp.concatenate(values, 1)), 0)
    table = dot_nt(peers, values)
    spread(table[:, 0:128] + table[:, 128:256] + table[:, 256:384], half, send_ref, 1)
    for dy, join in ((1, first_of), (-1, last_of)):
        for dx, near_row, far_row in ((1, 127, 126), (-1, 0, 1)):
            to_x = bx + dx
            to_y = by + dy
            corner = join(
                ice_ref[SIDE_Y + near_row : SIDE_Y + near_row + 1],
                ice_ref[SIDE_Y + far_row : SIDE_Y + far_row + 1],
            )
            corner = pltpu.roll(jnp.where(flat < 72, corner, 0.0), 40, 1)

            @pl.when((to_x >= 0) & (to_x < 16) & (to_y >= 0) & (to_y < 16))
            def _():
                at = to_x * 16 + to_y
                send_ref[pl.ds(at, 1), :] = send_ref[pl.ds(at, 1), :] + corner


def bulk_kernel(
    state_ref, lo_ref, hi_ref, left_ref, right_ref, weight_ref, top_ref, out_ref, wide_ref,
):
    lane = iota((8, 128), 1)
    outer = (lane & 4) == 0

    for k in range(90):
        wide_ref[8 * k : 8 * k + 8] = jnp.broadcast_to(weight_ref[k : k + 1], (8, 128))

    def weight(k):
        return wide_ref[8 * k : 8 * k + 8]

    def group(g, carry):
        at = pl.multiple_of(g * 64, 64)
        far = pl.multiple_of(g * 32, 32)
        side = pl.multiple_of(8 * g, 8)
        x = [lo_ref[pl.ds(far + r, 8, stride=4), :] for r in range(4)]
        x = x + [state_ref[pl.ds(at + r, 8, stride=8), :] for r in range(8)]
        x = x + [hi_ref[pl.ds(far + r, 8, stride=4), :] for r in range(4)]
        own = jnp.zeros((8, 128), F32)
        for p in range(16):
            own = jnp.where((lane >> 3) == p, pltpu.roll(x[p], (8 * p + 4) % 128, 1), own)
        near = whole_side(
            merged(left_ref[pl.ds(side, 8), :], right_ref[pl.ds(side, 8), :]),
            lo_ref[pl.ds(pl.multiple_of(side + DEEP, 8), 8), :],
            hi_ref[pl.ds(pl.multiple_of(side + DEEP, 8), 8), :],
        )
        strips = [jnp.where(outer, own, near), jnp.where(outer, near, own)]
        for substep in range(NSUB):
            ends = jnp.where((lane & 7) == 4, strips[0], strips[1])
            new = [None] * 16
            for p in range(substep + 1, 15 - substep):
                end = pltpu.roll(ends, (128 - 8 * p - 4) % 128, 1)
                here = x[p]
                after = pltpu.roll(jnp.where(lane == 0, end, here), 127, 1)
                before = pltpu.roll(jnp.where(lane == 127, end, here), 1, 1)
                y = weight(64 + p) * here + weight(p) * x[p + 1] + weight(16 + p) * x[p - 1]
                new[p] = y + weight(32 + p) * after + weight(48 + p) * before
            if substep + 1 < NSUB:
                moved = []
                for k in range(2):
                    s = strips[k]
                    y = weight(88 + k) * s + weight(80 + k) * pltpu.roll(s, 120, 1)
                    y = y + weight(82 + k) * pltpu.roll(s, 8, 1)
                    moved.append(y + weight(84 + k) * pltpu.roll(s, 127, 1) + weight(86 + k) * pltpu.roll(s, 1, 1))
                strips = moved
            x = new
        for r in range(8):
            out_ref[pl.ds(at + r, 8, stride=8), :] = x[r + 4]
        return carry

    lax.fori_loop(0, 30, group, 0, unroll=2)
    for f in range(4):
        out_ref[480 * f : 480 * f + 8] = top_ref[8 * f : 8 * f + 8]


def two_sum(a, b):
    s = a + b
    t = s - a
    return s, (a - (s - t)) + (b - t)


def two_product(a, b):
    def split(v):
        c = 4097.0 * v
        high = c - (c - v)
        return high, v - high

    p = a * b
    a1, a2 = split(a)
    b1, b2 = split(b)
    return p, ((a1 * b1 - p) + a1 * b2 + a2 * b1) + a2 * b2


def add_pair(a, b):
    s, e = two_sum(a[0], b[0])
    e = e + (a[1] + b[1])
    return two_sum(s, e)


def less_scaled(a, k, b):
    p, e = two_product(k, b[0])
    return add_pair(a, (-p, -(e + k * b[1])))


def fold(pair, axis, sizes):
    for size in sizes:
        turned = tuple(pltpu.roll(v, size, axis) for v in pair)
        pair = add_pair(pair, turned)
    return pair


def tiles_sum(x, low=None):
    total = x[0:8]
    error = jnp.zeros((8, 128), F32) if low is None else low[0:8]
    for r in range(8, x.shape[0], 8):
        total, e = two_sum(total, x[r : r + 8])
        error = error + e
        if low is not None:
            error = error + low[r : r + 8]
    return fold(two_sum(total, error), 0, (4, 2, 1))


def ice_kernel(
    owner_ref, table_ref, lo_ref, hi_ref, left_ref, right_ref,
    thick, visc, fric, ground, coup, drive, guess, nodemap_ref,
    send_ref, res_ref, z_ref, y_ref, w_ref, v_ref,
):
    half, half_lo, half_hi = halves()
    _, bx, by = place_of()
    flat = iota((1, 128), 1)

    def corner_from(x, y):
        ok = (x >= 0) & (x < 16) & (y >= 0) & (y < 16)
        got = pltpu.roll(table_ref[pl.ds(jnp.where(ok, x * 16 + y, 0), 1), :], 88, 1)
        return jnp.where(ok & (flat < 72), got, 0.0)

    def corners_at(x):
        from_left = corner_from(x, by - 1)
        from_right = corner_from(x, by + 1)
        return (
            merged(from_left, pltpu.roll(from_right, 4, 1)),
            merged(pltpu.roll(from_left, 124, 1), from_right),
        )

    lo_near, lo_far = corners_at(bx - 1)
    hi_near, hi_far = corners_at(bx + 1)
    side = merged(left_ref[SIDE_Y : SIDE_Y + 128], right_ref[SIDE_Y : SIDE_Y + 128])
    gap = jnp.zeros((4, 128), F32)
    side = jnp.concatenate([side, hi_near, hi_far, gap, lo_far, lo_near], 0)
    gets = ice_fields((thick, visc, fric, ground, coup, drive, guess))
    gets = gets + (lambda at: nodemap_ref[...],)
    lane = iota((136, 128), 1)
    edge = (lane < 4) | (lane >= 124)

    def padded(a):
        at = LEAD + 4 * a
        centre = jnp.concatenate([gets[a](WHOLE), hi_ref[at : at + 4], lo_ref[at : at + 4]], 0)
        edges = jnp.where(edge, pltpu.roll(side, (128 - 8 * a - 4) % 128, 1), 0.0)
        return jnp.concatenate([centre, edges], 1)

    table = table_ref[...]
    mine = table_ref[pl.ds(pl.multiple_of(half * 128, 128), 128), :]
    node = columns_of(owner_ref)
    lane = iota((128, 128), 1)
    rows = []
    cols = []
    for s in range(4):
        column = node[:, s : s + 1]
        rows.append(onehot(lane == (column >> 7)))
        cols.append(jnp.where(lane == (column & 127), mine[:, 16 + s : 17 + s], 0.0))
    cols = jnp.concatenate(split3(jnp.concatenate(cols, 0)), 1)
    melt = dot_tn(jnp.concatenate(rows, 0), cols)
    melt = melt[:, 0:128] + melt[:, 128:256] + melt[:, 256:384]

    code = padded(8)
    row = iota((136, 256), 0)
    col = iota((136, 256), 1)
    half_at = jnp.where(row < 128, half, jnp.where(row < 132, half_hi, half_lo))
    dx = jnp.where(row < 128, 1, jnp.where(row < 132, 2, 0))
    dy = jnp.where(col < 128, 1, jnp.where(col < 192, 2, 0))
    owner, lane_of = decode(code, half_at, 3 * dx + dy)
    parts = table_parts(table)
    rim = [
        lookup(parts, owner[r : r + 1, :128], lane_of[r : r + 1, :128]) for r in range(128, 136)
    ]
    side_owner = (owner[:, 128:] + 1).astype(F32)
    side_lane = lane_of[:, 128:].astype(F32)
    spare = jnp.zeros((8, 128), F32)
    sides = []
    for block in range(9):
        if block < 8:
            piece_owner = side_owner[16 * block : 16 * block + 16]
            piece_lane = side_lane[16 * block : 16 * block + 16]
        else:
            piece_owner = jnp.concatenate([side_owner[128:136], spare], 0)
            piece_lane = jnp.concatenate([side_lane[128:136], spare], 0)
        at_owner = pack_rows(piece_owner).astype(I32) - 1
        at_lane = pack_rows(piece_lane).astype(I32)
        piece = unpack_rows(lookup(parts, at_owner, at_lane))
        sides.append(piece if block < 8 else piece[0:8])
    melt = jnp.concatenate([melt] + rim, 0)
    melt = jnp.concatenate([melt, jnp.concatenate(sides, 0)], 1)

    thickness = padded(0)
    inside = thickness > 0.0
    thinned = thickness * jnp.exp(-0.3 * melt)
    depth = padded(1) * thinned
    base = padded(2) + 0.2
    cross = 0.9 * base * padded(3)
    w_e = 0.5 * (depth + turn(depth, -1, 0))
    w_w = 0.5 * (depth + turn(depth, 1, 0))
    w_n = 0.5 * (depth + turn(depth, -1, 1))
    w_s = 0.5 * (depth + turn(depth, 1, 1))
    diagonal = w_e + w_w + w_n + w_s + base
    inverse = jnp.where(inside, 1.0 / diagonal, 0.0)

    def apply(pair):
        out = []
        for a in range(2):
            x = pair[a]
            beside = w_e * turn(x, -1, 0) + w_w * turn(x, 1, 0)
            beside = beside + w_n * turn(x, -1, 1) + w_s * turn(x, 1, 1)
            out.append(diagonal * x - beside + cross * pair[1 - a])
        return out

    first = [padded(6), padded(7)]
    image = apply(first)
    res = [padded(4 + a) * thinned - image[a] for a in range(2)]
    z = [res[a] * inverse for a in range(2)]
    y = apply(z)
    w = [y[a] * inverse for a in range(2)]
    v = apply(w)
    inner = (slice(0, 128), slice(0, 128))
    lane = iota((256, 128), 1)
    message = jnp.zeros((256, 128), F32)
    for k, (one, two) in enumerate(((res, z), (z, y), (y, w), (w, v))):
        product = jnp.concatenate([one[a][inner] * two[a][inner] for a in range(2)], 0)
        pair = fold(tiles_sum(product), 1, (64, 32, 16, 8, 4, 2, 1))
        message = jnp.where(lane == k, pair[0][0:1], message)
        message = jnp.where(lane == k + 4, pair[1][0:1], message)
    send_ref[...] = message
    for a in range(2):
        res_ref[a] = res[a][inner]
        z_ref[a] = z[a][inner]
        y_ref[a] = y[a][inner]
        w_ref[a] = w[a][inner]
        v_ref[a] = v[a][inner]


def update_kernel(sum_ref, guess_ref, res_ref, z_ref, y_ref, w_ref, v_ref, vel_ref, left_ref):
    got = sum_ref[...]
    pair = tiles_sum(got, pltpu.roll(got, 124, 1))
    norm, curve, mixed, far = ((pair[0][0:1, k : k + 1], pair[1][0:1, k : k + 1]) for k in range(4))
    step = norm[0] / curve[0]
    rest = less_scaled(norm, step, curve)
    along = less_scaled(curve, step, mixed)
    norm_next = (rest[0] - step * along[0]) + (rest[1] - step * along[1])
    ratio = norm_next / norm[0]
    curve_next = less_scaled(along, step, less_scaled(mixed, step, far))[0]
    curve_next = curve_next + 2.0 * ratio * along[0] + ratio * ratio * curve[0]
    step_next = norm_next / curve_next
    one = step + step_next * (1.0 + ratio)
    two = step_next * step
    for a in range(2):
        vel_ref[a] = guess_ref[a] + one * z_ref[a] - two * w_ref[a]
        left_ref[a] = res_ref[a] - one * y_ref[a] + two * v_ref[a]


def sds(*shape):
    return jax.ShapeDtypeStruct(shape, F32)


SMALL = 24 << 20


def call(kernel, outs, *args, stay=(), limit=None, **kw):
    args = [x if any(x is y for y in stay) else here(x) for x in args]
    vmem = pl.BlockSpec(memory_space=pltpu.VMEM)
    return pl.pallas_call(
        kernel,
        in_specs=[vmem] * len(args),
        out_specs=[vmem] * len(outs),
        out_shape=outs,
        compiler_params=pltpu.CompilerParams(vmem_limit_bytes=limit),
        **kw,
    )(*args)


def block(*shape):
    return pl.BlockSpec(shape, lambda i: (0,) * len(shape))


def here(x):
    return pltpu.with_memory_space_constraint(x, pltpu.VMEM)


def swap(up, down, axes):
    size = lax.axis_size(axes)
    forward = [(i, i + 1) for i in range(size - 1)]
    low = lax.ppermute(up, axes, forward)
    high = lax.ppermute(down, axes, [(b, a) for a, b in forward])
    return here(low), here(high)


def exchange(table):
    return here(lax.all_to_all(table, ALL, split_axis=0, concat_axis=0, tiled=True))


def shards(
    ocean_state, diffusivity, wet_mask, coast_column, coast_slot, owner_node,
    thickness, viscosity, friction, grounded, coupling, driving, first_guess,
):
    owner = owner_node[0, 0].T
    columns = coast_column.reshape(1, 256)
    slots = coast_slot.reshape(1, 256)
    ice = (thickness, viscosity, friction, grounded, coupling, driving, first_guess)
    state = ocean_state.reshape(1920, 128)
    given = (state, diffusivity, wet_mask, columns, slots, owner) + ice

    send_draft, lead = pl.pallas_call(
        draft_kernel,
        name="draft",
        grid=(1,),
        in_specs=[block(4, 128), block(128, 128), block(4, 1, 8, 128), block(8, 128), block(8, 128)]
        + [block(1, 256), block(1, 256)],
        out_specs=[block(512, 128), block(64, 128)],
        out_shape=[sds(512, 128), sds(64, 128)],
    )(owner, thickness, ocean_state, diffusivity, wet_mask, columns, slots)
    got_draft = exchange(send_draft)
    up, down, nodemap = call(
        pack_x_kernel,
        [sds(64, 128), sds(64, 128), sds(128, 128)],
        lead, owner, *ice,
        stay=given + (lead,),
        limit=SMALL,
    )
    lo, hi = swap(up, down, XAXES)
    (side,) = call(
        pack_y_kernel,
        [sds(SIDE_Y + 128, 128)],
        state, nodemap, *ice,
        stay=given,
        limit=SMALL,
    )
    left, right = swap(side, side, GY)
    up, down = call(
        pack_deep_kernel,
        [sds(DEEP + 240, 128), sds(DEEP + 240, 128)],
        state, left, right,
        stay=given,
        limit=SMALL,
    )
    deep_lo, deep_hi = swap(up, down, XAXES)

    top, melt_mean, weights, send_melt = call(
        top_kernel,
        [sds(32, 128), sds(8, 128), sds(96, 128), sds(256, 128)],
        lead, lo, hi, got_draft, side,
        scratch_shapes=[pltpu.VMEM((128, 128), F32)],
        limit=SMALL,
    )
    got_melt = exchange(send_melt)
    (fields,) = call(
        bulk_kernel,
        [sds(1920, 128)],
        state, deep_lo, deep_hi, left, right, weights, top,
        stay=given + (weights, top),
        limit=SMALL,
        scratch_shapes=[pltpu.VMEM((720, 128), F32)],
    )

    pair = sds(2, 128, 128)
    send_sums, res, z, y, w, v = call(
        ice_kernel,
        [sds(256, 128), pair, pair, pair, pair, pair],
        owner, got_melt, lo, hi, left, right, *ice, nodemap,
    )
    got_sums = exchange(send_sums)
    pair = sds(2, 128, 128)
    velocity, residual = call(
        update_kernel, [pair, pair], got_sums, first_guess, res, z, y, w, v,
        stay=(first_guess, res, z, y, w, v), limit=SMALL,
    )
    return (fields.reshape(ocean_state.shape), melt_mean, velocity, residual)


def solution(mesh):
    split = Mesh(
        mesh.devices.reshape(mesh.shape["grp"], mesh.shape["gx"], 4, 4),
        ("grp", "gx", "gy_0", "gy_1"),
    )
    field = P(("grp", "gx"), GY)
    pair = P(None, ("grp", "gx"), GY)
    levels = P(None, None, ("grp", "gx"), GY)
    lists = P(("grp", "gx"), GY, None)
    placed = (levels, field, field, lists, lists, P(("grp", "gx"), GY, None, None))
    placed = placed + (field,) * 5 + (pair, pair)
    return jax.shard_map(
        shards,
        mesh=split,
        in_specs=placed,
        out_specs=(levels, field, pair, pair),
        check_vma=False,
    )
```

```python
import jax
import jax.numpy as jnp
from jax import lax
from jax.experimental import pallas as pl
from jax.experimental.pallas import tpu as pltpu
from jax.sharding import Mesh
from jax.sharding import PartitionSpec as P


NSUB = 4
GY = ("gy_0", "gy_1")
XAXES = ("grp", "gx")
ALL = ("grp", "gx", "gy_0", "gy_1")
LEAD = 24
DEEP = 960
SIDE_Y = 240
F32 = jnp.float32
BF16 = jnp.bfloat16
I32 = jnp.int32


def iota(shape, dim):
    return lax.broadcasted_iota(I32, shape, dim)


def split3(x):
    high = x.astype(BF16)
    rest = x - high.astype(F32)
    mid = rest.astype(BF16)
    low = (rest - mid.astype(F32)).astype(BF16)
    return high, mid, low


def onehot(hit):
    return jnp.where(hit, 1.0, 0.0).astype(BF16)


def dot_tn(a, b):
    return lax.dot_general(a, b, (((0,), (0,)), ((), ())), preferred_element_type=F32)


def dot_nt(a, b):
    return lax.dot_general(a, b, (((1,), (1,)), ((), ())), preferred_element_type=F32)


def spread(table, half, out_ref, stride):
    row = iota((128, 128), 0) & 15
    group = iota((128, 128), 1) >> 2
    after = pltpu.roll(table, 127, 0)
    before = pltpu.roll(table, 1, 0)
    parts = []
    for dx in range(3):
        part = jnp.where((group == 3 * dx) & (row > 0), before, 0.0)
        part = jnp.where(group == 3 * dx + 1, table, part)
        part = jnp.where((group == 3 * dx + 2) & (row < 15), after, part)
        parts.append(part)
    none = jnp.zeros((16, 128), F32)
    own = parts[1] + jnp.concatenate([none, parts[0][:112]], 0)
    own = own + jnp.concatenate([parts[2][16:], none], 0)
    first = jnp.where(half == 0, parts[0][112:], 0.0)
    last = jnp.where(half == 1, parts[2][:16], 0.0)
    other = jnp.concatenate([first, jnp.zeros((96, 128), F32), last], 0)
    size = 128 * stride
    if stride > 1:
        out_ref[...] = jnp.zeros(out_ref.shape, F32)
    out_ref[pl.ds(pl.multiple_of(half * size, size), 128, stride=stride), :] = own
    out_ref[pl.ds(pl.multiple_of((1 - half) * size, size), 128, stride=stride), :] = other


def place_of():
    half = lax.axis_index("grp")
    bx = half * 8 + lax.axis_index("gx")
    by = lax.axis_index("gy_0") * 4 + lax.axis_index("gy_1")
    return half, bx, by


def first_of(near, far):
    return jnp.where((iota(near.shape, 1) & 4) == 0, near, pltpu.roll(far, 4, 1))


def last_of(near, far):
    return jnp.where((iota(near.shape, 1) & 4) == 0, pltpu.roll(near, 124, 1), far)


def columns_of(owner_ref):
    node = owner_ref[...].astype(F32)
    return jnp.transpose(jnp.concatenate([node, node], 0)).astype(I32)


def draft_kernel(owner_ref, thick_ref, state_ref, diff_ref, wet_ref, col_ref, slot_ref, out_ref, lead_ref):
    half, bx, by = place_of()
    lane = iota((128, 128), 1)
    parts = split3(thick_ref[...])
    node = columns_of(owner_ref)
    table = jnp.zeros((128, 128), F32)
    for s in range(4):
        column = node[:, s : s + 1]
        pick = onehot(lane == (column >> 7))
        rows = jnp.dot(pick, parts[0], preferred_element_type=F32)
        rows = rows + jnp.dot(pick, parts[1], preferred_element_type=F32)
        rows = rows + jnp.dot(pick, parts[2], preferred_element_type=F32)
        value = jnp.sum(jnp.where(lane == (column & 127), rows, 0.0), 1, keepdims=True)
        table = jnp.where((lane & 3) == s, 0.9 * value, table)
    spread(table, half, out_ref, 2)

    col = col_ref[...]
    slot = slot_ref[...]
    hit = iota((8, 256), 0) == (col >> 7)
    peer = jnp.where(hit, ((slot >> 2) + 1).astype(F32), 0.0)
    which = jnp.where(hit, (slot & 3).astype(F32), 0.0)
    lanes = onehot(iota((128, 256), 0) == (col & 127))
    both = dot_nt(jnp.concatenate([peer, which], 0).astype(BF16), lanes)
    for f in range(4):
        lead_ref[8 * f : 8 * f + 8] = state_ref[f, 0]
    lead_ref[32:40] = jnp.where(wet_ref[...] > 0, diff_ref[...], 0.0)
    lead_ref[40:48] = jnp.where(both[:8] > 0.5, 4.0 * both[:8] + both[8:] - 3.0, 0.0)
    lead_ref[48:64] = jnp.zeros((16, 128), F32)
    side = edges(lambda r: lead_ref[pl.ds(r, 8, stride=8), :])
    flat = iota((1, 128), 1)
    for dy, join in ((1, first_of), (-1, last_of)):
        pairs = [join(side[2 * j : 2 * j + 1], side[2 * j + 1 : 2 * j + 2]) for j in range(3)]
        one = jnp.where(flat >= 64, pltpu.roll(pairs[2], 32, 1), 0.0)
        two = jnp.where(flat < 64, pltpu.roll(pairs[0], 96, 1), pltpu.roll(pairs[1], 32, 1))
        for dx in (-1, 0, 1):
            to_x = bx + dx
            to_y = by + dy

            @pl.when((to_x >= 0) & (to_x < 16) & (to_y >= 0) & (to_y < 16))
            def _():
                at = 2 * (to_x * 16 + to_y)
                out_ref[pl.ds(at, 1), :] = out_ref[pl.ds(at, 1), :] + one
                out_ref[pl.ds(at + 1, 1), :] = two


def edges(get):
    place = iota((8, 128), 1) >> 3
    acc = jnp.zeros((8, 128), F32)
    for r in range(8):
        acc = jnp.where(place == r + 4, pltpu.roll(get(r), (8 * (r + 4) + 4) % 128, 1), acc)
    return acc


def ice_fields(refs):
    thick, visc, fric, ground, coup, drive, guess = refs
    return (
        lambda at: thick[at],
        lambda at: visc[at],
        lambda at: fric[at] * ground[at].astype(F32),
        lambda at: coup[at],
        lambda at: drive[(0,) + at],
        lambda at: drive[(1,) + at],
        lambda at: guess[(0,) + at],
        lambda at: guess[(1,) + at],
    )


WHOLE = (slice(None), slice(None))


def pack_y_kernel(
    state_ref, nodemap_ref,
    thick, visc, fric, ground, coup, drive, guess,
    side_ref,
):
    def group(g, carry):
        at = pl.multiple_of(g * 64, 64)
        side_ref[pl.ds(pl.multiple_of(8 * g, 8), 8), :] = edges(
            lambda r: state_ref[pl.ds(at + r, 8, stride=8), :]
        )
        return carry

    lax.fori_loop(0, 30, group, 0, unroll=2)

    gets = ice_fields((thick, visc, fric, ground, coup, drive, guess))
    gets = gets + (lambda at: nodemap_ref[...],)
    place = iota((128, 128), 1) >> 3
    acc = jnp.zeros((128, 128), F32)
    for a, get in enumerate(gets):
        acc = jnp.where(place == a, pltpu.roll(get(WHOLE), 8 * a + 4, 1), acc)
    side_ref[SIDE_Y : SIDE_Y + 128] = acc


def merged(left, right):
    return jnp.where((iota(left.shape, 1) & 4) == 0, left, right)


def pack_x_kernel(
    lead_ref, owner_ref,
    thick, visc, fric, ground, coup, drive, guess,
    up_ref, down_ref, nodemap_ref,
):
    node = columns_of(owner_ref)
    lane = iota((128, 128), 1)
    number = iota((128, 128), 0).astype(F32) + 1.0
    peers = []
    whichs = []
    cols = []
    for s in range(4):
        column = node[:, s : s + 1]
        hit = lane == (column >> 7)
        peers.append(jnp.where(hit, number, 0.0).astype(BF16))
        whichs.append(jnp.where(hit, float(s), 0.0).astype(BF16))
        cols.append(onehot(lane == (column & 127)))
    cols = jnp.concatenate(cols, 0)
    peer = dot_tn(jnp.concatenate(peers, 0), cols)
    which = dot_tn(jnp.concatenate(whichs, 0), cols)
    nodemap_ref[...] = jnp.where(peer > 0.5, 4.0 * peer + which - 3.0, 0.0)

    for i in range(6):
        up_ref[4 * i : 4 * i + 4] = lead_ref[8 * i + 4 : 8 * i + 8]
        down_ref[4 * i : 4 * i + 4] = lead_ref[8 * i : 8 * i + 4]
    top = (pl.ds(0, 4), slice(None))
    end = (pl.ds(124, 4), slice(None))
    gets = ice_fields((thick, visc, fric, ground, coup, drive, guess))
    gets = gets + (lambda at: nodemap_ref[at],)
    for a, get in enumerate(gets):
        up_ref[LEAD + 4 * a : LEAD + 4 * a + 4] = get(end)
        down_ref[LEAD + 4 * a : LEAD + 4 * a + 4] = get(top)
    up_ref[60:64] = jnp.zeros((4, 128), F32)
    down_ref[60:64] = jnp.zeros((4, 128), F32)


def pack_deep_kernel(state_ref, left_ref, right_ref, up_ref, down_ref):
    def group(g, carry):
        at = pl.multiple_of(g * 64, 64)
        to = pl.multiple_of(g * 32, 32)
        for r in range(4):
            up_ref[pl.ds(to + r, 8, stride=4), :] = state_ref[pl.ds(at + 4 + r, 8, stride=8), :]
            down_ref[pl.ds(to + r, 8, stride=4), :] = state_ref[pl.ds(at + r, 8, stride=8), :]
        return carry

    lax.fori_loop(0, 30, group, 0, unroll=2)
    side = merged(left_ref[0:SIDE_Y], right_ref[0:SIDE_Y])
    up_ref[DEEP : DEEP + 240] = side
    down_ref[DEEP : DEEP + 240] = side


def whole_side(own, lo, hi):
    lane = iota(own.shape, 1)
    far = pltpu.roll(jnp.where(lane < 64, hi, lo), 64, 1)
    return jnp.where((lane < 32) | (lane >= 96), far, own)


def turn(x, shift, axis):
    return pltpu.roll(x, shift % x.shape[axis], axis)


def lookup(parts, owner, lane_of):
    pick = onehot(iota((256, 128), 0) == owner)
    found = jnp.dot(parts, pick, preferred_element_type=F32)
    found = found[0:48] + found[48:96] + found[96:144]
    return jnp.sum(jnp.where(iota((48, 128), 0) == lane_of, found, 0.0), 0, keepdims=True)


def table_parts(table):
    turned = jnp.transpose(table)[0:48]
    return jnp.concatenate(split3(turned), 0)


def decode(code, half, group):
    number = code.astype(I32) - 1
    owner = jnp.where(number >= 0, half * 128 + (number >> 2), -1)
    return owner, 4 * group + (number & 3)


def pack_rows(x):
    lane = iota((16, 128), 1)
    moved = jnp.where(lane < 8, pltpu.roll(x, 4, 1), 0.0)
    moved = pltpu.roll(moved, 0, 1, stride=8, stride_axis=0)
    return jnp.sum(moved, 0, keepdims=True)


def unpack_rows(row):
    lane = iota((16, 128), 1)
    turned = [row] + [pltpu.roll(row, 128 - 8 * r, 1) for r in range(1, 16)]
    moved = jnp.where(lane < 8, jnp.concatenate(turned, 0), 0.0)
    return pltpu.roll(moved, 124, 1)


def halves():
    half = lax.axis_index("grp")
    bx = half * 8 + lax.axis_index("gx")
    return half, jnp.maximum(bx - 1, 0) >> 3, jnp.minimum(bx + 1, 15) >> 3


def top_kernel(
    lead_ref, lo_ref, hi_ref, table_ref, ice_ref,
    top_ref, melt_ref, weight_ref, send_ref, turn_ref,
):
    half, half_lo, half_hi = halves()
    _, bx, by = place_of()
    flat = iota((1, 128), 1)

    def pairs_from(x, y):
        ok = (x >= 0) & (x < 16) & (y >= 0) & (y < 16)
        at = jnp.where(ok, 2 * (x * 16 + y), 0)
        one = table_ref[pl.ds(at, 1), :]
        two = table_ref[pl.ds(at + 1, 1), :]
        found = (pltpu.roll(two, 32, 1), pltpu.roll(two, 96, 1), pltpu.roll(one, 96, 1))
        return [jnp.where(ok & (flat >= 32) & (flat < 96), f, 0.0) for f in found]

    def columns_at(x):
        from_left = pairs_from(x, by - 1)
        from_right = pairs_from(x, by + 1)
        rows = []
        for j in range(3):
            rows.append(merged(from_left[j], pltpu.roll(from_right[j], 4, 1)))
            rows.append(merged(pltpu.roll(from_left[j], 124, 1), from_right[j]))
        return jnp.concatenate(rows + [jnp.zeros((2, 128), F32)], 0)

    side = whole_side(columns_at(bx), columns_at(bx - 1), columns_at(bx + 1))
    for c in range(16):
        p = (c + 4) % 16
        turn_ref[8 * c : 8 * c + 8] = pltpu.roll(side, (128 - 8 * p - 4) % 128, 1)
    lane = iota((16, 128), 1)
    edge = (lane < 4) | (lane >= 124)

    def padded(i):
        centre = jnp.concatenate(
            [lead_ref[8 * i : 8 * i + 8], hi_ref[4 * i : 4 * i + 4], lo_ref[4 * i : 4 * i + 4]], 0
        )
        edges = jnp.where(edge, turn_ref[pl.ds(i, 16, stride=8), :], 0.0)
        return jnp.concatenate([centre, edges], 1)

    fields = [padded(f) for f in range(4)]
    diff = padded(4)
    code = padded(5)
    weights = []
    for axis, shift in ((0, -1), (0, 1), (1, -1), (1, 1)):
        other = turn(diff, shift, axis)
        weights.append(jnp.where((diff > 0.0) & (other > 0.0), 0.5 * (diff + other), 0.0))
    keep = 1.0 - (weights[0] + weights[1] + weights[2] + weights[3])
    for j, w in enumerate(weights + [keep]):
        centre = w[:, 0:128]
        weight_ref[16 * j : 16 * j + 12] = jnp.concatenate([w[12:16, 0:128], w[0:8, 0:128]], 0)
        weight_ref[16 * j + 12 : 16 * j + 16] = w[8:12, 0:128]
        east = jnp.where(lane < 4, pltpu.roll(centre, 4, 1), pltpu.roll(w[:, 128:256], 4, 1))
        west = jnp.where(lane < 4, pltpu.roll(w[:, 128:256], 4, 1), pltpu.roll(centre, 4, 1))
        for k, strip in enumerate((east, west)):
            strip = jnp.where(lane < 8, strip, 0.0)
            strip = jnp.sum(pltpu.roll(strip, 0, 1, stride=8, stride_axis=0), 0, keepdims=True)
            weight_ref[80 + 2 * j + k : 81 + 2 * j + k] = pltpu.roll(strip, 32, 1)
    weight_ref[90:96] = jnp.zeros((6, 128), F32)

    row = iota((16, 128), 0)
    half_at = jnp.where(row < 8, half, jnp.where(row < 12, half_hi, half_lo))
    dx = jnp.where(row < 8, 1, jnp.where(row < 12, 2, 0))
    owner, lane_of = decode(code[:, 0:128], half_at, 3 * dx + 1)
    place = flat >> 3
    half_at = jnp.where(place < 4, half_lo, jnp.where(place < 12, half, half_hi))
    dx = jnp.where(place < 4, 0, jnp.where(place < 12, 1, 2))
    dy = jnp.where((flat & 4) == 0, 0, 2)
    side_owner, side_lane = decode(side[5:6], half_at, 3 * dx + dy)
    parts = table_parts(table_ref[pl.ds(0, 256, stride=2), :])
    none = jnp.zeros((1, 128), F32)
    found = [
        none if r in (11, 12) else lookup(parts, owner[r : r + 1], lane_of[r : r + 1]) for r in range(16)
    ]
    side_found = lookup(parts, side_owner, side_lane)
    turned = []
    for c in range(16):
        p = (c + 4) % 16
        turned.append(pltpu.roll(side_found, (128 - 8 * p - 4) % 128, 1))
    edges = jnp.where(edge, jnp.concatenate(turned, 0), 0.0)
    draft = jnp.concatenate([jnp.concatenate(found, 0), edges], 1)
    cover = jnp.where(code > 0.5, 1.0, 0.0)

    total = jnp.zeros((8, 128), F32)
    for _ in range(NSUB):
        temp, salt, east, north = fields
        speed = jnp.sqrt(east * east + north * north + 0.01)
        freezing = -0.5 * salt + 0.3 * draft - 0.2
        melt = 0.5 * cover * (temp - freezing) * speed
        drag = 0.05 * cover * speed
        total = total + melt[0:8, 0:128]
        loss = (0.3 * melt, 0.2 * melt, drag * east, drag * north)
        changed = []
        for f in range(4):
            x = fields[f]
            flux = weights[0] * (turn(x, -1, 0) - x) + weights[1] * (turn(x, 1, 0) - x)
            flux = flux + weights[2] * (turn(x, -1, 1) - x) + weights[3] * (turn(x, 1, 1) - x)
            changed.append(x + flux - loss[f])
        fields = changed
    for f in range(4):
        top_ref[8 * f : 8 * f + 8] = fields[f][0:8, 0:128]
    mean = total * (1.0 / NSUB)
    melt_ref[...] = mean

    number = lead_ref[40:48].astype(I32) - 1
    peers = []
    values = []
    for r in range(8):
        at = number[r : r + 1]
        peers.append(onehot(iota((128, 128), 0) == (at >> 2)))
        values.append(jnp.where((iota((128, 128), 0) & 3) == (at & 3), mean[r : r + 1], 0.0))
    peers = jnp.concatenate(peers, 1)
    values = jnp.concatenate(split3(jnp.concatenate(values, 1)), 0)
    table = dot_nt(peers, values)
    spread(table[:, 0:128] + table[:, 128:256] + table[:, 256:384], half, send_ref, 1)
    for dy, join in ((1, first_of), (-1, last_of)):
        for dx, near_row, far_row in ((1, 127, 126), (-1, 0, 1)):
            to_x = bx + dx
            to_y = by + dy
            corner = join(
                ice_ref[SIDE_Y + near_row : SIDE_Y + near_row + 1],
                ice_ref[SIDE_Y + far_row : SIDE_Y + far_row + 1],
            )
            corner = pltpu.roll(jnp.where(flat < 72, corner, 0.0), 40, 1)

            @pl.when((to_x >= 0) & (to_x < 16) & (to_y >= 0) & (to_y < 16))
            def _():
                at = to_x * 16 + to_y
                send_ref[pl.ds(at, 1), :] = send_ref[pl.ds(at, 1), :] + corner


def bulk_kernel(
    state_ref, lo_ref, hi_ref, left_ref, right_ref, weight_ref, top_ref, out_ref, wide_ref,
):
    lane = iota((8, 128), 1)
    outer = (lane & 4) == 0

    for k in range(90):
        wide_ref[8 * k : 8 * k + 8] = jnp.broadcast_to(weight_ref[k : k + 1], (8, 128))

    def weight(k):
        return wide_ref[8 * k : 8 * k + 8]

    def group(g, carry):
        at = pl.multiple_of(g * 64, 64)
        far = pl.multiple_of(g * 32, 32)
        side = pl.multiple_of(8 * g, 8)
        x = [lo_ref[pl.ds(far + r, 8, stride=4), :] for r in range(4)]
        x = x + [state_ref[pl.ds(at + r, 8, stride=8), :] for r in range(8)]
        x = x + [hi_ref[pl.ds(far + r, 8, stride=4), :] for r in range(4)]
        own = jnp.zeros((8, 128), F32)
        for p in range(16):
            own = jnp.where((lane >> 3) == p, pltpu.roll(x[p], (8 * p + 4) % 128, 1), own)
        near = whole_side(
            merged(left_ref[pl.ds(side, 8), :], right_ref[pl.ds(side, 8), :]),
            lo_ref[pl.ds(pl.multiple_of(side + DEEP, 8), 8), :],
            hi_ref[pl.ds(pl.multiple_of(side + DEEP, 8), 8), :],
        )
        strips = [jnp.where(outer, own, near), jnp.where(outer, near, own)]
        for substep in range(NSUB):
            ends = jnp.where((lane & 7) == 4, strips[0], strips[1])
            new = [None] * 16
            for p in range(substep + 1, 15 - substep):
                end = pltpu.roll(ends, (128 - 8 * p - 4) % 128, 1)
                here = x[p]
                after = pltpu.roll(jnp.where(lane == 0, end, here), 127, 1)
                before = pltpu.roll(jnp.where(lane == 127, end, here), 1, 1)
                y = weight(64 + p) * here + weight(p) * x[p + 1] + weight(16 + p) * x[p - 1]
                new[p] = y + weight(32 + p) * after + weight(48 + p) * before
            if substep + 1 < NSUB:
                moved = []
                for k in range(2):
                    s = strips[k]
                    y = weight(88 + k) * s + weight(80 + k) * pltpu.roll(s, 120, 1)
                    y = y + weight(82 + k) * pltpu.roll(s, 8, 1)
                    moved.append(y + weight(84 + k) * pltpu.roll(s, 127, 1) + weight(86 + k) * pltpu.roll(s, 1, 1))
                strips = moved
            x = new
        for r in range(8):
            out_ref[pl.ds(at + r, 8, stride=8), :] = x[r + 4]
        return carry

    lax.fori_loop(0, 30, group, 0, unroll=2)
    for f in range(4):
        out_ref[480 * f : 480 * f + 8] = top_ref[8 * f : 8 * f + 8]


def two_sum(a, b):
    s = a + b
    t = s - a
    return s, (a - (s - t)) + (b - t)


def two_product(a, b):
    def split(v):
        c = 4097.0 * v
        high = c - (c - v)
        return high, v - high

    p = a * b
    a1, a2 = split(a)
    b1, b2 = split(b)
    return p, ((a1 * b1 - p) + a1 * b2 + a2 * b1) + a2 * b2


def add_pair(a, b):
    s, e = two_sum(a[0], b[0])
    e = e + (a[1] + b[1])
    return two_sum(s, e)


def less_scaled(a, k, b):
    p, e = two_product(k, b[0])
    return add_pair(a, (-p, -(e + k * b[1])))


def fold(pair, axis, sizes):
    for size in sizes:
        turned = tuple(pltpu.roll(v, size, axis) for v in pair)
        pair = add_pair(pair, turned)
    return pair


def tiles_sum(x, low=None):
    total = x[0:8]
    error = jnp.zeros((8, 128), F32) if low is None else low[0:8]
    for r in range(8, x.shape[0], 8):
        total, e = two_sum(total, x[r : r + 8])
        error = error + e
        if low is not None:
            error = error + low[r : r + 8]
    return fold(two_sum(total, error), 0, (4, 2, 1))


def ice_kernel(
    owner_ref, table_ref, lo_ref, hi_ref, left_ref, right_ref,
    thick, visc, fric, ground, coup, drive, guess, nodemap_ref,
    send_ref, res_ref, z_ref, y_ref, w_ref, v_ref,
):
    half, half_lo, half_hi = halves()
    _, bx, by = place_of()
    flat = iota((1, 128), 1)

    def corner_from(x, y):
        ok = (x >= 0) & (x < 16) & (y >= 0) & (y < 16)
        got = pltpu.roll(table_ref[pl.ds(jnp.where(ok, x * 16 + y, 0), 1), :], 88, 1)
        return jnp.where(ok & (flat < 72), got, 0.0)

    def corners_at(x):
        from_left = corner_from(x, by - 1)
        from_right = corner_from(x, by + 1)
        return (
            merged(from_left, pltpu.roll(from_right, 4, 1)),
            merged(pltpu.roll(from_left, 124, 1), from_right),
        )

    lo_near, lo_far = corners_at(bx - 1)
    hi_near, hi_far = corners_at(bx + 1)
    side = merged(left_ref[SIDE_Y : SIDE_Y + 128], right_ref[SIDE_Y : SIDE_Y + 128])
    gap = jnp.zeros((4, 128), F32)
    side = jnp.concatenate([side, hi_near, hi_far, gap, lo_far, lo_near], 0)
    gets = ice_fields((thick, visc, fric, ground, coup, drive, guess))
    gets = gets + (lambda at: nodemap_ref[...],)
    lane = iota((136, 128), 1)
    edge = (lane < 4) | (lane >= 124)

    def padded(a):
        at = LEAD + 4 * a
        centre = jnp.concatenate([gets[a](WHOLE), hi_ref[at : at + 4], lo_ref[at : at + 4]], 0)
        edges = jnp.where(edge, pltpu.roll(side, (128 - 8 * a - 4) % 128, 1), 0.0)
        return jnp.concatenate([centre, edges], 1)

    table = table_ref[...]
    mine = table_ref[pl.ds(pl.multiple_of(half * 128, 128), 128), :]
    node = columns_of(owner_ref)
    lane = iota((128, 128), 1)
    rows = []
    cols = []
    for s in range(4):
        column = node[:, s : s + 1]
        rows.append(onehot(lane == (column >> 7)))
        cols.append(jnp.where(lane == (column & 127), mine[:, 16 + s : 17 + s], 0.0))
    cols = jnp.concatenate(split3(jnp.concatenate(cols, 0)), 1)
    melt = dot_tn(jnp.concatenate(rows, 0), cols)
    melt = melt[:, 0:128] + melt[:, 128:256] + melt[:, 256:384]

    code = padded(8)
    row = iota((136, 256), 0)
    col = iota((136, 256), 1)
    half_at = jnp.where(row < 128, half, jnp.where(row < 132, half_hi, half_lo))
    dx = jnp.where(row < 128, 1, jnp.where(row < 132, 2, 0))
    dy = jnp.where(col < 128, 1, jnp.where(col < 192, 2, 0))
    owner, lane_of = decode(code, half_at, 3 * dx + dy)
    parts = table_parts(table)
    unused = jnp.zeros((1, 128), F32)
    rim = [
        unused if r in (131, 132) else lookup(parts, owner[r : r + 1, :128], lane_of[r : r + 1, :128])
        for r in range(128, 136)
    ]
    side_owner = (owner[:, 128:] + 1).astype(F32)
    side_lane = lane_of[:, 128:].astype(F32)
    spare = jnp.zeros((8, 128), F32)
    sides = []
    for block in range(9):
        if block < 8:
            piece_owner = side_owner[16 * block : 16 * block + 16]
            piece_lane = side_lane[16 * block : 16 * block + 16]
        else:
            piece_owner = jnp.concatenate([side_owner[128:136], spare], 0)
            piece_lane = jnp.concatenate([side_lane[128:136], spare], 0)
        at_owner = pack_rows(piece_owner).astype(I32) - 1
        at_lane = pack_rows(piece_lane).astype(I32)
        piece = unpack_rows(lookup(parts, at_owner, at_lane))
        sides.append(piece if block < 8 else piece[0:8])
    melt = jnp.concatenate([melt] + rim, 0)
    melt = jnp.concatenate([melt, jnp.concatenate(sides, 0)], 1)

    thickness = padded(0)
    inside = thickness > 0.0
    thinned = thickness * jnp.exp(-0.3 * melt)
    depth = padded(1) * thinned
    base = padded(2) + 0.2
    cross = 0.9 * base * padded(3)
    w_e = 0.5 * (depth + turn(depth, -1, 0))
    w_w = 0.5 * (depth + turn(depth, 1, 0))
    w_n = 0.5 * (depth + turn(depth, -1, 1))
    w_s = 0.5 * (depth + turn(depth, 1, 1))
    diagonal = w_e + w_w + w_n + w_s + base
    inverse = jnp.where(inside, 1.0 / diagonal, 0.0)

    def apply(pair):
        out = []
        for a in range(2):
            x = pair[a]
            beside = w_e * turn(x, -1, 0) + w_w * turn(x, 1, 0)
            beside = beside + w_n * turn(x, -1, 1) + w_s * turn(x, 1, 1)
            out.append(diagonal * x - beside + cross * pair[1 - a])
        return out

    first = [padded(6), padded(7)]
    image = apply(first)
    res = [padded(4 + a) * thinned - image[a] for a in range(2)]
    z = [res[a] * inverse for a in range(2)]
    y = apply(z)
    w = [y[a] * inverse for a in range(2)]
    v = apply(w)
    inner = (slice(0, 128), slice(0, 128))
    lane = iota((256, 128), 1)
    message = jnp.zeros((256, 128), F32)
    for k, (one, two) in enumerate(((res, z), (z, y), (y, w), (w, v))):
        product = jnp.concatenate([one[a][inner] * two[a][inner] for a in range(2)], 0)
        pair = fold(tiles_sum(product), 1, (64, 32, 16, 8, 4, 2, 1))
        message = jnp.where(lane == k, pair[0][0:1], message)
        message = jnp.where(lane == k + 4, pair[1][0:1], message)
    send_ref[...] = message
    for a in range(2):
        res_ref[a] = res[a][inner]
        z_ref[a] = z[a][inner]
        y_ref[a] = y[a][inner]
        w_ref[a] = w[a][inner]
        v_ref[a] = v[a][inner]


def update_kernel(sum_ref, guess_ref, res_ref, z_ref, y_ref, w_ref, v_ref, vel_ref, left_ref):
    got = sum_ref[...]
    pair = tiles_sum(got, pltpu.roll(got, 124, 1))
    norm, curve, mixed, far = ((pair[0][0:1, k : k + 1], pair[1][0:1, k : k + 1]) for k in range(4))
    step = norm[0] / curve[0]
    rest = less_scaled(norm, step, curve)
    along = less_scaled(curve, step, mixed)
    norm_next = (rest[0] - step * along[0]) + (rest[1] - step * along[1])
    ratio = norm_next / norm[0]
    curve_next = less_scaled(along, step, less_scaled(mixed, step, far))[0]
    curve_next = curve_next + 2.0 * ratio * along[0] + ratio * ratio * curve[0]
    step_next = norm_next / curve_next
    one = step + step_next * (1.0 + ratio)
    two = step_next * step
    for a in range(2):
        vel_ref[a] = guess_ref[a] + one * z_ref[a] - two * w_ref[a]
        left_ref[a] = res_ref[a] - one * y_ref[a] + two * v_ref[a]


def sds(*shape):
    return jax.ShapeDtypeStruct(shape, F32)


SMALL = 24 << 20


def near(*shape):
    return pltpu.VMEM(shape, F32)


def call(kernel, outs, *args, stay=(), limit=None, **kw):
    args = [x if any(x is y for y in stay) else here(x) for x in args]
    vmem = pl.BlockSpec(memory_space=pltpu.VMEM)
    return pl.pallas_call(
        kernel,
        in_specs=[vmem] * len(args),
        out_specs=[vmem] * len(outs),
        out_shape=outs,
        compiler_params=pltpu.CompilerParams(vmem_limit_bytes=limit),
        **kw,
    )(*args)


def block(*shape):
    return pl.BlockSpec(shape, lambda i: (0,) * len(shape))


def here(x):
    return pltpu.with_memory_space_constraint(x, pltpu.VMEM)


def swap(up, down, axes):
    size = lax.axis_size(axes)
    forward = [(i, i + 1) for i in range(size - 1)]
    low = lax.ppermute(up, axes, forward)
    high = lax.ppermute(down, axes, [(b, a) for a, b in forward])
    return here(low), here(high)


def exchange(table):
    return here(lax.all_to_all(table, ALL, split_axis=0, concat_axis=0, tiled=True))


def shards(
    ocean_state, diffusivity, wet_mask, coast_column, coast_slot, owner_node,
    thickness, viscosity, friction, grounded, coupling, driving, first_guess,
):
    owner = owner_node[0, 0].T
    columns = coast_column.reshape(1, 256)
    slots = coast_slot.reshape(1, 256)
    ice = (thickness, viscosity, friction, grounded, coupling, driving, first_guess)
    state = ocean_state.reshape(1920, 128)
    given = (state, diffusivity, wet_mask, columns, slots, owner) + ice

    send_draft, lead = pl.pallas_call(
        draft_kernel,
        name="draft",
        grid=(1,),
        in_specs=[block(4, 128), block(128, 128), block(4, 1, 8, 128), block(8, 128), block(8, 128)]
        + [block(1, 256), block(1, 256)],
        out_specs=[block(512, 128), block(64, 128)],
        out_shape=[sds(512, 128), near(64, 128)],
    )(owner, thickness, ocean_state, diffusivity, wet_mask, columns, slots)
    got_draft = exchange(send_draft)
    up, down, nodemap = call(
        pack_x_kernel,
        [sds(64, 128), sds(64, 128), sds(128, 128)],
        lead, owner, *ice,
        stay=given,
        limit=SMALL,
    )
    lo, hi = swap(up, down, XAXES)
    (side,) = call(
        pack_y_kernel,
        [sds(SIDE_Y + 128, 128)],
        state, nodemap, *ice,
        stay=given,
        limit=SMALL,
    )
    left, right = swap(side, side, GY)
    up, down = call(
        pack_deep_kernel,
        [sds(DEEP + 240, 128), sds(DEEP + 240, 128)],
        state, left, right,
        stay=given,
        limit=SMALL,
    )
    deep_lo, deep_hi = swap(up, down, XAXES)

    top, melt_mean, weights, send_melt = call(
        top_kernel,
        [sds(32, 128), sds(8, 128), sds(96, 128), sds(256, 128)],
        lead, lo, hi, got_draft, side,
        scratch_shapes=[pltpu.VMEM((128, 128), F32)],
        limit=SMALL,
    )
    got_melt = exchange(send_melt)
    (fields,) = call(
        bulk_kernel,
        [sds(1920, 128)],
        state, deep_lo, deep_hi, left, right, weights, top,
        stay=given + (weights, top),
        limit=SMALL,
        scratch_shapes=[pltpu.VMEM((720, 128), F32)],
    )

    pair = sds(2, 128, 128)
    send_sums, res, z, y, w, v = call(
        ice_kernel,
        [sds(256, 128), pair, pair, pair, pair, pair],
        owner, got_melt, lo, hi, left, right, *ice, nodemap,
    )
    got_sums = exchange(send_sums)
    pair = sds(2, 128, 128)
    velocity, residual = call(
        update_kernel, [pair, pair], got_sums, first_guess, res, z, y, w, v,
        stay=(first_guess, res, z, y, w, v), limit=SMALL,
    )
    return (fields.reshape(ocean_state.shape), melt_mean, velocity, residual)


def solution(mesh):
    split = Mesh(
        mesh.devices.reshape(mesh.shape["grp"], mesh.shape["gx"], 4, 4),
        ("grp", "gx", "gy_0", "gy_1"),
    )
    field = P(("grp", "gx"), GY)
    pair = P(None, ("grp", "gx"), GY)
    levels = P(None, None, ("grp", "gx"), GY)
    lists = P(("grp", "gx"), GY, None)
    placed = (levels, field, field, lists, lists, P(("grp", "gx"), GY, None, None))
    placed = placed + (field,) * 5 + (pair, pair)
    return jax.shard_map(
        shards,
        mesh=split,
        in_specs=placed,
        out_specs=(levels, field, pair, pair),
        check_vma=False,
    )
```
